32 devices in a mesh: fsdp: 32 (over z, y, x, core).
Axes of the slice: x: 2, y: 2, z: 4, core: 2. Of those that a mesh axis runs over, the one named last changes fastest.
Arguments:
- inputs: bfloat16 [32, 128, 768], P('fsdp'), may hold values from -6 to 6
- encoded: bfloat16 [32, 64, 768], P('fsdp')
- lengths: int32 [32], P('fsdp'), may hold values from 32 to 128, as said below
- bucket_ids: int32 [128], replicated, may hold values from 0 to 31, as said below
- qkv_weights: bfloat16 [768, 6, 768], P('fsdp')
- out_weights: bfloat16 [768, 2, 768], P('fsdp'), may hold values from -1.75 to 1.75
- ff_in: bfloat16 [768, 2, 2048], P('fsdp'), may hold values from -0.21875 to 0.21875
- ff_out: bfloat16 [2048, 768], P('fsdp'), may hold values from -0.125 to 0.125
- gains: bfloat16 [3, 768], P(None, 'fsdp'), may hold values from 0.5 to 1.5
- bias_table: float32 [32, 12], replicated
- cotangent: bfloat16 [32, 128, 768], P('fsdp'), may hold values from -6 to 6
Outputs:
- outputs: bfloat16 [32, 128, 768], P('fsdp')
- input_grad: bfloat16 [32, 128, 768], P('fsdp')
- encoded_grad: bfloat16 [32, 64, 768], P('fsdp')
- qkv_grad: float32 [768, 6, 768], P('fsdp')
- out_grad: float32 [768, 2, 768], P('fsdp')
- ffin_grad: float32 [768, 2, 2048], P('fsdp')
- ffout_grad: float32 [2048, 768], P('fsdp')
- gain_grad: float32 [3, 768], P(None, 'fsdp')
- table_grad: float32 [32, 12], replicated
The draws below stay inside these ranges and needn't reach their ends.
Inputs may be any that keep to these rules, and one draw needn't show every extreme that they name: `lengths`: some sequence uses all 128 slots. `bucket_ids`: non-decreasing in the distance; distance 0 has bucket 0 and distance 128 - 1 bucket 32 - 1.
All inputs are finite; a program needn't handle non-finite values.
Results may differ from the reference program's by a relative error of at most 0.02.
Values may be sent and summed in bfloat16 or wider, within the bound.
A program may use at most 192 MiB of HBM per device.

```python
import jax
import jax.numpy as jnp
from jax import lax

D = 768
HEADS = 12
HEAD = 64
FF = 2048
NB = 32
L = 128
E = 64
SEQS = 32


def draw_lengths(key, part):
    values = jax.random.randint(key, (SEQS,), L // 4, L + 1).astype(jnp.int32)
    return values.at[0].set(L)


def draw_bucket_ids(key, part):
    steps = jax.random.randint(key, (L,), 0, 2).astype(jnp.int32)
    steps = steps.at[0].set(0)
    buckets = jnp.minimum(jnp.cumsum(steps), NB - 1).astype(jnp.int32)
    return buckets.at[L - 1].set(NB - 1)


def draw_qkv_weights(key, part):
    values = jnp.clip(jax.random.normal(key, (D, 6, D), jnp.float32), -6.0, 6.0)
    which = jnp.arange(6, dtype=jnp.int32)
    query_like = (which == 0) | (which == 3)
    factor = jnp.where(query_like, (D * HEAD) ** (-0.5), D ** (-0.5)).astype(jnp.float32)
    return (values * factor[None, :, None]).astype(jnp.bfloat16)


def draw_encoded(key, part):
    values = jnp.clip(jax.random.normal(key, (SEQS, E, D), jnp.float32), -6.0, 6.0)
    return values.astype(jnp.bfloat16)


def draw_bias_table(key, part):
    values = jnp.clip(jax.random.normal(key, (NB, HEADS), jnp.float32), -4.0, 4.0)
    return values.astype(jnp.float32)


def block_scale(rng, dims, pieces, low, top_value):
    level = 1.0
    for position, parts in pieces:
        steps = jax.random.uniform(jax.random.fold_in(jax.random.fold_in(rng, 6), position), (parts,), jnp.float32, low / len(pieces), top_value / len(pieces))
        level = level * jnp.repeat(jnp.exp(steps), dims[position] // parts).reshape((-1,) + (1,) * (len(dims) - 1 - position))
    return level


def bell_draw(key, dims, width, most, shards=(), kind=jnp.bfloat16):
    values = width * jax.random.normal(key, dims, jnp.float32)
    if shards:
        values = values * block_scale(key, dims, shards, -0.22, 0.18)
    return jnp.clip(values, -most, most).astype(kind)


def setup_inputs(seed: int = 0) -> dict:
    streams_of = jax.random.split(jax.random.key(seed), 12)
    inputs = bell_draw(streams_of[0], (SEQS, L, D), 1.0, 6.0, ((0, 32),))
    encoded = draw_encoded(jax.random.fold_in(streams_of[11], 71), 0)
    lengths = draw_lengths(jax.random.fold_in(streams_of[11], 71), 0)
    bucket_ids = draw_bucket_ids(jax.random.fold_in(streams_of[11], 71), 0)
    qkv_weights = draw_qkv_weights(jax.random.fold_in(streams_of[11], 71), 0)
    out_weights = bell_draw(streams_of[5], (D, 2, D), (D // 64) ** -0.5, 1.75, ((0, 32),))
    ff_in = bell_draw(streams_of[6], (D, 2, FF), D ** -0.5, 0.21875, ((0, 32),))
    ff_out = bell_draw(streams_of[7], (FF, D), FF ** -0.5, 0.125, ((0, 32),))
    gains = jnp.clip(1.0 + 0.1 * jax.random.normal(streams_of[8], (3, D), jnp.float32), 0.5, 1.5).astype(jnp.bfloat16)
    bias_table = draw_bias_table(jax.random.fold_in(streams_of[11], 71), 0)
    cotangent = bell_draw(streams_of[10], (SEQS, L, D), 1.0, 6.0, ((0, 32),))
    return {"inputs": inputs, "encoded": encoded, "lengths": lengths, "bucket_ids": bucket_ids, "qkv_weights": qkv_weights, "out_weights": out_weights, "ff_in": ff_in, "ff_out": ff_out, "gains": gains, "bias_table": bias_table, "cotangent": cotangent}


EPS = 1e-06

def prod(form, left, right):
    return jnp.einsum(form, left.astype(jnp.float32), right.astype(jnp.float32))

def gelu_tanh(value):
    return 0.5 * value * (1.0 + jnp.tanh(0.7978845608028654 * (value + 0.044715 * value * value * value)))

def rms_fwd(value, gain):
    recip = lax.rsqrt(lax.optimization_barrier(jnp.mean(value * value, axis=-1, keepdims=True)) + EPS)
    normed = value * recip
    return ((normed * gain).astype(jnp.bfloat16), normed, recip)

def rms_bwd(grad, normed, recip, gain):
    scaled = grad * gain
    gain_grad = lax.optimization_barrier(jnp.sum(grad * normed, axis=0))
    back = recip * (scaled - normed * lax.optimization_barrier(jnp.mean(scaled * normed, axis=-1, keepdims=True)))
    return (back, gain_grad)

def scores_of(query, keys, bias, mask):
    rows = query.shape[0]
    q3 = query.reshape(rows, -1, HEAD)
    k3 = keys.reshape(keys.shape[0], -1, HEAD)
    scores = prod('qhd,khd->hqk', q3, k3)
    if bias is not None:
        scores = scores + bias
    if mask is not None:
        scores = jnp.where(mask[None], scores, -1e+30)
    return scores

def attend(query, keys, values, bias, mask, shifted):
    rows = query.shape[0]
    scores = scores_of(query, keys, bias, mask)
    if shifted:
        top = lax.optimization_barrier(jnp.max(scores, axis=-1, keepdims=True))
        lse = top + jnp.log(lax.optimization_barrier(jnp.sum(jnp.exp(scores - top), axis=-1, keepdims=True)))
    else:
        lse = jnp.log(lax.optimization_barrier(jnp.sum(jnp.exp(scores), axis=-1, keepdims=True)))
    prob = jnp.exp(scores - lse).astype(jnp.bfloat16)
    v3 = values.reshape(values.shape[0], -1, HEAD)
    out = prod('hqk,khd->qhd', prob, v3).reshape(rows, -1).astype(jnp.bfloat16)
    return (out, lse)

def attend_back(query, keys, values, out, lse, grad_out, bias, mask):
    rows = query.shape[0]
    scores = scores_of(query, keys, bias, mask)
    prob = jnp.exp(scores - lse)
    prob_b = prob.astype(jnp.bfloat16)
    q3 = query.reshape(rows, -1, HEAD)
    k3 = keys.reshape(keys.shape[0], -1, HEAD)
    v3 = values.reshape(values.shape[0], -1, HEAD)
    grad3 = grad_out.reshape(rows, -1, HEAD)
    grad_b = grad3.astype(jnp.bfloat16)
    out3 = out.reshape(rows, -1, HEAD).astype(jnp.float32)
    d_val = prod('hqk,qhd->khd', prob_b, grad_b)
    d_prob = prod('qhd,khd->hqk', grad_b, v3)
    delta = jnp.transpose(lax.optimization_barrier(jnp.sum(grad3 * out3, axis=2)), (1, 0))
    d_score = prob * (d_prob - delta[:, :, None])
    d_score_b = d_score.astype(jnp.bfloat16)
    d_query = prod('hqk,khd->qhd', d_score_b, k3)
    d_key = prod('hqk,qhd->khd', d_score_b, q3)
    shape_q = (rows, -1)
    shape_k = (keys.shape[0], -1)
    return (d_query.reshape(shape_q).astype(jnp.bfloat16), d_key.reshape(shape_k).astype(jnp.bfloat16), d_val.reshape(shape_k).astype(jnp.bfloat16), d_score)

def forward(rows, enc, length, bucket_ids, weights, table):
    qkv_w, out_w, ff_in, ff_out, gains = weights
    seq = rows.shape[0]
    gain_f = gains.astype(jnp.float32)
    start = rows.astype(jnp.float32)
    h1, n1, r1 = rms_fwd(start, gain_f[0])
    qkv = prod('ld,dce->cle', h1, qkv_w[:, 0:3]).astype(jnp.bfloat16)
    row_ids = lax.broadcasted_iota(jnp.int32, (seq, seq), 0)
    col_ids = lax.broadcasted_iota(jnp.int32, (seq, seq), 1)
    dist = jnp.maximum(row_ids - col_ids, 0)
    mask = (col_ids <= row_ids) & (col_ids < length)
    onehot = (bucket_ids[:, None] == jnp.arange(table.shape[0], dtype=jnp.int32)[None, :]).astype(jnp.float32)
    bias_dist = jnp.dot(onehot, table, precision=lax.Precision.HIGHEST)
    bias = jnp.transpose(bias_dist[dist], (2, 0, 1))
    a1, lse1 = attend(qkv[0], qkv[1], qkv[2], bias, mask, True)
    x1 = start + prod('le,ed->ld', a1, out_w[:, 0])
    h2, n2, r2 = rms_fwd(x1, gain_f[1])
    qc = prod('ld,de->le', h2, qkv_w[:, 3]).astype(jnp.bfloat16)
    kvc = prod('ld,dce->cle', enc, qkv_w[:, 4:6]).astype(jnp.bfloat16)
    ac, lse2 = attend(qc, kvc[0], kvc[1], None, None, False)
    x2 = x1 + prod('le,ed->ld', ac, out_w[:, 1])
    h3, n3, r3 = rms_fwd(x2, gain_f[2])
    gate_up = prod('ld,dcf->clf', h3, ff_in)
    hidden = (gelu_tanh(gate_up[0]) * gate_up[1]).astype(jnp.bfloat16)
    result = x2 + prod('lf,fd->ld', hidden, ff_out)
    saved = (h1, n1, r1, qkv, bias, mask, a1, lse1, h2, n2, r2, qc, kvc, ac, lse2, h3, n3, r3, gate_up, hidden, onehot, dist)
    return (result.astype(jnp.bfloat16), saved)

def ff_back(saved, weights, cot):
    qkv_w, out_w, ff_in, ff_out, gains = weights
    gain_f = gains.astype(jnp.float32)
    h3, n3, r3, gate_up, hidden = (saved[15], saved[16], saved[17], saved[18], saved[19])
    d_ffout = prod('lf,ld->fd', hidden, cot)
    d_hidden = prod('ld,fd->lf', cot, ff_out)
    gelu_val, gelu_pull = jax.vjp(gelu_tanh, gate_up[0])
    d_gate = gelu_pull(d_hidden * gate_up[1])[0]
    d_up = d_hidden * gelu_val
    d_gate_up = jnp.stack([d_gate, d_up]).astype(jnp.bfloat16)
    d_ffin = prod('ld,clf->dcf', h3, d_gate_up)
    d_h3 = prod('clf,dcf->ld', d_gate_up, ff_in)
    back3, gain3 = rms_bwd(d_h3, n3, r3, gain_f[2])
    return (cot.astype(jnp.float32) + back3, d_ffin, d_ffout, gain3)

def cross_back(saved, weights, enc, dx2):
    qkv_w, out_w, ff_in, ff_out, gains = weights
    gain_f = gains.astype(jnp.float32)
    h2, n2, r2, qc, kvc, ac, lse2 = (saved[8], saved[9], saved[10], saved[11], saved[12], saved[13], saved[14])
    dx2_b = dx2.astype(jnp.bfloat16)
    d_outc = prod('le,ld->ed', ac, dx2_b)
    d_ac = prod('ld,ed->le', dx2_b, out_w[:, 1])
    d_qc, d_kc, d_vc, unused = attend_back(qc, kvc[0], kvc[1], ac, lse2, d_ac, None, None)
    g_qc = prod('ld,le->de', h2, d_qc)
    d_kvc = jnp.stack([d_kc, d_vc])
    g_kvc = prod('ld,cle->dce', enc, d_kvc)
    enc_grad = prod('cle,dce->ld', d_kvc, qkv_w[:, 4:6]).astype(jnp.bfloat16)
    d_h2 = prod('le,de->ld', d_qc, qkv_w[:, 3])
    back2, gain2 = rms_bwd(d_h2, n2, r2, gain_f[1])
    return (dx2 + back2, g_qc, g_kvc, d_outc, gain2, enc_grad)

def self_back(saved, weights, dx1):
    qkv_w, out_w, ff_in, ff_out, gains = weights
    gain_f = gains.astype(jnp.float32)
    h1, n1, r1, qkv, bias, mask, a1, lse1 = saved[0:8]
    onehot, dist = (saved[20], saved[21])
    seq = h1.shape[0]
    dx1_b = dx1.astype(jnp.bfloat16)
    d_outs = prod('le,ld->ed', a1, dx1_b)
    d_a1 = prod('ld,ed->le', dx1_b, out_w[:, 0])
    d_q, d_k, d_v, d_score = attend_back(qkv[0], qkv[1], qkv[2], a1, lse1, d_a1, bias, mask)
    d_qkv = jnp.stack([d_q, d_k, d_v])
    g_qkv = prod('ld,cle->dce', h1, d_qkv)
    d_h1 = prod('cle,dce->ld', d_qkv, qkv_w[:, 0:3])
    back1, gain1 = rms_bwd(d_h1, n1, r1, gain_f[0])
    flat = jnp.transpose(d_score, (1, 2, 0)).reshape(seq * seq, -1)
    d_dist = jax.ops.segment_sum(flat, dist.reshape(-1), num_segments=seq)
    d_table = jnp.dot(onehot.T, d_dist, precision=lax.Precision.HIGHEST)
    return ((dx1 + back1).astype(jnp.bfloat16), g_qkv, d_outs, gain1, d_table)

def reference(inputs, encoded, lengths, bucket_ids, qkv_weights, out_weights, ff_in, ff_out, gains, bias_table, cotangent):
    weights = (qkv_weights, out_weights, ff_in, ff_out, gains)

    def one(carry, item):
        rows, enc, length, cot = item
        result, saved = forward(rows, enc, length, bucket_ids, weights, bias_table)
        dx2, g_ffin, g_ffout, gain3 = ff_back(saved, weights, cot)
        dx1, g_qc, g_kvc, g_outc, gain2, enc_grad = cross_back(saved, weights, enc, dx2)
        dx, g_qkvs, g_outs, gain1, g_table = self_back(saved, weights, dx1)
        g_qkv = jnp.concatenate([g_qkvs, g_qc[:, None], g_kvc], axis=1)
        g_out = jnp.stack([g_outs, g_outc], axis=1)
        g_gain = jnp.stack([gain1, gain2, gain3])
        terms = (g_qkv, g_out, g_ffin, g_ffout, g_gain, g_table)
        carry = tuple((c + t for c, t in zip(carry, terms)))
        return (carry, (result, dx, enc_grad))
    zeros = (jnp.zeros(qkv_weights.shape, jnp.float32), jnp.zeros(out_weights.shape, jnp.float32), jnp.zeros(ff_in.shape, jnp.float32), jnp.zeros(ff_out.shape, jnp.float32), jnp.zeros(gains.shape, jnp.float32), jnp.zeros(bias_table.shape, jnp.float32))
    totals, per_seq = lax.scan(one, zeros, (inputs, encoded, lengths, cotangent))
    outputs, input_grad, encoded_grad = per_seq
    return (outputs, input_grad, encoded_grad, totals[0], totals[1], totals[2], totals[3], totals[4], totals[5])
```

```python
import functools

import jax
import jax.numpy as jnp
from jax import lax
from jax.experimental import pallas as pl
from jax.experimental.pallas import tpu as pltpu
from jax.sharding import PartitionSpec as P

HEAD = 64


EPS = 1e-06


def prod(form, left, right):
    return jnp.einsum(form, left, right, preferred_element_type=jnp.float32)


def gelu_tanh(value):
    return (
        0.5
        * value
        * (1.0 + jnp.tanh(0.7978845608028654 * (value + 0.044715 * value * value * value)))
    )


def rms_fwd(value, gain):
    recip = lax.rsqrt(jnp.mean(value * value, axis=-1, keepdims=True) + EPS)
    normed = value * recip
    return ((normed * gain).astype(jnp.bfloat16), normed, recip)


def rms_bwd(grad, normed, recip, gain):
    scaled = grad * gain
    gain_grad = jnp.sum(grad * normed, axis=0)
    back = recip * (scaled - normed * jnp.mean(scaled * normed, axis=-1, keepdims=True))
    return (back, gain_grad)


def toeplitz_bias(bucket_ids, table, positions):
    onehot = (bucket_ids[:, None] == jnp.arange(table.shape[0], dtype=jnp.int32)[None, :]).astype(
        jnp.float32
    )
    by_dist = jnp.transpose(jnp.dot(onehot, table, precision=lax.Precision.HIGHEST), (1, 0))
    head_count = by_dist.shape[0]
    nearest = jnp.broadcast_to(by_dist[:, 0:1], (head_count, positions))
    cyclic = jnp.concatenate(
        [nearest, jnp.zeros((head_count, 1), jnp.float32), by_dist[:, :0:-1]], axis=1
    )
    tiled = jnp.broadcast_to(cyclic[:, None, :], (head_count, positions, 2 * positions))
    tiled = tiled.reshape(head_count, 2 * positions * positions)
    skewed = tiled[:, : positions * (2 * positions - 1)].reshape(
        head_count, positions, 2 * positions - 1
    )
    return (skewed[:, :, :positions], onehot)


def diagonal_sums(d_score, onehot):
    head_count, positions = (d_score.shape[0], d_score.shape[1])
    padded = jnp.pad(d_score, ((0, 0), (0, 0), (0, positions - 1)))
    padded = padded.reshape(head_count, positions * (2 * positions - 1))
    padded = jnp.pad(padded, ((0, 0), (0, positions))).reshape(head_count, positions, 2 * positions)
    column = jnp.sum(padded, axis=1)
    by_dist = jnp.concatenate(
        [jnp.sum(column[:, :positions], axis=1, keepdims=True), column[:, :positions:-1]], axis=1
    )
    return jnp.dot(
        jnp.transpose(onehot, (1, 0)),
        jnp.transpose(by_dist, (1, 0)),
        precision=lax.Precision.HIGHEST,
    )


def scores_of(query, keys, bias, mask):
    rows = query.shape[0]
    q3 = query.reshape(rows, -1, HEAD)
    k3 = keys.reshape(keys.shape[0], -1, HEAD)
    scores = prod("qhd,khd->hqk", q3, k3)
    if bias is not None:
        scores = scores + bias
    if mask is not None:
        scores = jnp.where(mask[None], scores, -1e30)
    return scores


def attend(query, keys, values, bias, mask, shifted):
    rows = query.shape[0]
    scores = scores_of(query, keys, bias, mask)
    if shifted:
        top = jnp.max(scores, axis=-1, keepdims=True)
        lse = top + jnp.log(jnp.sum(jnp.exp(scores - top), axis=-1, keepdims=True))
    else:
        lse = jnp.log(jnp.sum(jnp.exp(scores), axis=-1, keepdims=True))
    prob = jnp.exp(scores - lse).astype(jnp.bfloat16)
    v3 = values.reshape(values.shape[0], -1, HEAD)
    out = prod("hqk,khd->qhd", prob, v3).reshape(rows, -1).astype(jnp.bfloat16)
    return (out, lse)


def attend_back(query, keys, values, out, lse, grad_out, bias, mask):
    rows = query.shape[0]
    scores = scores_of(query, keys, bias, mask)
    prob = jnp.exp(scores - lse)
    prob_b = prob.astype(jnp.bfloat16)
    q3 = query.reshape(rows, -1, HEAD)
    k3 = keys.reshape(keys.shape[0], -1, HEAD)
    v3 = values.reshape(values.shape[0], -1, HEAD)
    grad3 = grad_out.reshape(rows, -1, HEAD)
    grad_b = grad3.astype(jnp.bfloat16)
    out3 = out.reshape(rows, -1, HEAD).astype(jnp.float32)
    d_val = prod("hqk,qhd->khd", prob_b, grad_b)
    d_prob = prod("qhd,khd->hqk", grad_b, v3)
    delta = jnp.transpose(jnp.sum(grad3 * out3, axis=2), (1, 0))
    d_score = prob * (d_prob - delta[:, :, None])
    d_score_b = d_score.astype(jnp.bfloat16)
    d_query = prod("hqk,khd->qhd", d_score_b, k3)
    d_key = prod("hqk,qhd->khd", d_score_b, q3)
    shape_q = (rows, -1)
    shape_k = (keys.shape[0], -1)
    return (
        d_query.reshape(shape_q).astype(jnp.bfloat16),
        d_key.reshape(shape_k).astype(jnp.bfloat16),
        d_val.reshape(shape_k).astype(jnp.bfloat16),
        d_score,
    )


def forward(rows, enc, length, bucket_ids, weights, table):
    qkv_w, out_w, ff_in, ff_out, gains = weights
    positions = rows.shape[0]
    gain_f = gains.astype(jnp.float32)
    start = rows.astype(jnp.float32)
    h1, n1, r1 = rms_fwd(start, gain_f[0])
    qkv = prod("ld,cde->cle", h1, qkv_w[0:3]).astype(jnp.bfloat16)
    row_ids = lax.broadcasted_iota(jnp.int32, (positions, positions), 0)
    col_ids = lax.broadcasted_iota(jnp.int32, (positions, positions), 1)
    mask = (col_ids <= row_ids) & (col_ids < length)
    bias, onehot = toeplitz_bias(bucket_ids, table, positions)
    a1, lse1 = attend(qkv[0], qkv[1], qkv[2], bias, mask, True)
    x1 = start + prod("le,ed->ld", a1, out_w[0])
    h2, n2, r2 = rms_fwd(x1, gain_f[1])
    qc = prod("ld,de->le", h2, qkv_w[3]).astype(jnp.bfloat16)
    kvc = prod("ld,cde->cle", enc, qkv_w[4:6]).astype(jnp.bfloat16)
    ac, lse2 = attend(qc, kvc[0], kvc[1], None, None, False)
    x2 = x1 + prod("le,ed->ld", ac, out_w[1])
    h3, n3, r3 = rms_fwd(x2, gain_f[2])
    gate_up = prod("ld,cdf->clf", h3, ff_in)
    hidden = (gelu_tanh(gate_up[0]) * gate_up[1]).astype(jnp.bfloat16)
    result = x2 + prod("lf,fd->ld", hidden, ff_out)
    saved = (
        h1,
        n1,
        r1,
        qkv,
        bias,
        mask,
        a1,
        lse1,
        h2,
        n2,
        r2,
        qc,
        kvc,
        ac,
        lse2,
        h3,
        n3,
        r3,
        gate_up,
        hidden,
        onehot,
    )
    return (result.astype(jnp.bfloat16), saved)


def ff_back(saved, weights, cot):
    qkv_w, out_w, ff_in, ff_out, gains = weights
    gain_f = gains.astype(jnp.float32)
    h3, n3, r3, gate_up, hidden = (saved[15], saved[16], saved[17], saved[18], saved[19])
    d_ffout = prod("lf,ld->fd", hidden, cot)
    d_hidden = prod("ld,fd->lf", cot, ff_out)
    gelu_val, gelu_pull = jax.vjp(gelu_tanh, gate_up[0])
    d_gate = gelu_pull(d_hidden * gate_up[1])[0]
    d_up = d_hidden * gelu_val
    d_gate_up = jnp.stack([d_gate, d_up]).astype(jnp.bfloat16)
    d_ffin = prod("ld,clf->cdf", h3, d_gate_up)
    d_h3 = prod("clf,cdf->ld", d_gate_up, ff_in)
    back3, gain3 = rms_bwd(d_h3, n3, r3, gain_f[2])
    return (cot.astype(jnp.float32) + back3, d_ffin, d_ffout, gain3)


def cross_back(saved, weights, enc, dx2):
    qkv_w, out_w, ff_in, ff_out, gains = weights
    gain_f = gains.astype(jnp.float32)
    h2, n2, r2, qc, kvc, ac, lse2 = (
        saved[8],
        saved[9],
        saved[10],
        saved[11],
        saved[12],
        saved[13],
        saved[14],
    )
    dx2_b = dx2.astype(jnp.bfloat16)
    d_outc = prod("le,ld->ed", ac, dx2_b)
    d_ac = prod("ld,ed->le", dx2_b, out_w[1])
    d_qc, d_kc, d_vc, unused = attend_back(qc, kvc[0], kvc[1], ac, lse2, d_ac, None, None)
    g_qc = prod("ld,le->de", h2, d_qc)
    d_kvc = jnp.stack([d_kc, d_vc])
    g_kvc = prod("ld,cle->cde", enc, d_kvc)
    enc_grad = prod("cle,cde->ld", d_kvc, qkv_w[4:6]).astype(jnp.bfloat16)
    d_h2 = prod("le,de->ld", d_qc, qkv_w[3])
    back2, gain2 = rms_bwd(d_h2, n2, r2, gain_f[1])
    return (dx2 + back2, g_qc, g_kvc, d_outc, gain2, enc_grad)


def self_back(saved, weights, dx1):
    qkv_w, out_w, ff_in, ff_out, gains = weights
    gain_f = gains.astype(jnp.float32)
    h1, n1, r1, qkv, bias, mask, a1, lse1 = saved[0:8]
    onehot = saved[20]
    dx1_b = dx1.astype(jnp.bfloat16)
    d_outs = prod("le,ld->ed", a1, dx1_b)
    d_a1 = prod("ld,ed->le", dx1_b, out_w[0])
    d_q, d_k, d_v, d_score = attend_back(qkv[0], qkv[1], qkv[2], a1, lse1, d_a1, bias, mask)
    d_qkv = jnp.stack([d_q, d_k, d_v])
    g_qkv = prod("ld,cle->cde", h1, d_qkv)
    d_h1 = prod("cle,cde->ld", d_qkv, qkv_w[0:3])
    back1, gain1 = rms_bwd(d_h1, n1, r1, gain_f[0])
    d_table = diagonal_sums(d_score, onehot)
    return ((dx1 + back1).astype(jnp.bfloat16), g_qkv, d_outs, gain1, d_table)


def to_blocks(array, width):
    blocks = []
    for copy in range(array.shape[0]):
        for start in range(0, array.shape[-1], width):
            block = array[copy, ..., start : start + width]
            short = width - block.shape[-1]
            if short:
                block = jnp.pad(block, ((0, 0),) * (block.ndim - 1) + ((0, short),))
            blocks.append(block)
    return blocks


def from_blocks(blocks, shape, width):
    copies, rows, columns = shape
    each = -(-columns // width)
    planes = []
    for copy in range(copies):
        part = [blocks[copy * each + at] for at in range(each)]
        part[-1] = part[-1][..., : columns - (each - 1) * width]
        planes.append(part[0] if each == 1 else jnp.concatenate(part, axis=-1))
    return planes


def plain_device(
    inputs,
    encoded,
    lengths,
    bucket_ids,
    qkv_weights,
    out_weights,
    ff_in,
    ff_out,
    gains,
    bias_table,
    cotangent,
):
    count = lax.axis_size("fsdp")
    shards = (
        jnp.transpose(qkv_weights, (1, 0, 2)),
        jnp.transpose(out_weights, (1, 0, 2)),
        jnp.transpose(ff_in, (1, 0, 2)),
        ff_out[None],
    )
    width = qkv_weights.shape[-1]
    depth = qkv_weights.shape[0]
    tall = ff_out.shape[0]
    blocks = to_blocks(shards[0], width) + to_blocks(shards[1], width) + to_blocks(shards[2], width)
    slots = gains.size
    tail = 8 * -(-slots // (8 * width))
    gain_rows = jnp.pad(gains.reshape(1, slots), ((0, 0), (0, tail * width - slots)))
    packed = jnp.concatenate(blocks + [ff_out, gain_rows.reshape(tail, width)], axis=0)
    whole = lax.all_gather(packed, "fsdp", axis=0, tiled=False)
    cut = len(blocks) * depth
    stacked = whole[:, :cut].reshape(count, len(blocks), depth, width)
    stacked = jnp.transpose(stacked, (1, 0, 2, 3)).reshape(len(blocks), count * depth, width)
    ff_out_all = whole[:, cut : cut + tall].reshape(count * tall, width)
    stacked, ff_out_all = lax.optimization_barrier((stacked, ff_out_all))
    n_qkv, n_out = qkv_weights.shape[1], out_weights.shape[1]
    ff_all = jnp.stack(from_blocks(stacked[n_qkv + n_out :], shards[2].shape, width))
    main = (stacked[:n_qkv], stacked[n_qkv : n_qkv + n_out], ff_all, ff_out_all[None])
    gain_all = whole[:, -tail:].reshape(count, tail * width)[:, :slots]
    gain_all = gain_all.reshape(count, gains.shape[0], gains.shape[1])
    gain_all = jnp.transpose(gain_all, (1, 0, 2)).reshape(gains.shape[0], -1)
    weights = (main[0], main[1], main[2], main[3][0], gain_all)
    result, saved = forward(inputs[0], encoded[0], lengths[0], bucket_ids, weights, bias_table)
    dx2, g_ffin, g_ffout, gain3 = ff_back(saved, weights, cotangent[0])
    dx1, g_qc, g_kvc, g_outc, gain2, enc_grad = cross_back(saved, weights, encoded[0], dx2)
    dx, g_qkvs, g_outs, gain1, g_table = self_back(saved, weights, dx1)
    wide = [g_qkvs[0], g_qkvs[1], g_qkvs[2], g_qc, g_kvc[0], g_kvc[1], g_outs, g_outc]
    wide += to_blocks(g_ffin, width)
    wide.append(g_ffout)
    g_gain = jnp.stack([gain1, gain2, gain3]).reshape(gains.shape[0], count, -1)
    g_gain = jnp.transpose(g_gain, (1, 0, 2)).reshape(count, slots)
    g_gain = jnp.pad(g_gain, ((0, 0), (0, tail * width - slots))).reshape(count, tail, width)
    parts = [grad.astype(jnp.bfloat16).reshape(count, -1, width) for grad in wide]
    send = jnp.concatenate(parts + [g_gain.astype(jnp.bfloat16)], axis=1)
    send, g_table = lax.optimization_barrier((send, g_table))
    own = lax.psum_scatter(send, "fsdp", scatter_dimension=0, tiled=False).astype(jnp.float32)
    mine = own[:cut].reshape(len(blocks), depth, width)
    s_ffin = jnp.stack(from_blocks(mine[n_qkv + n_out :], shards[2].shape, width))
    s_main = (mine[:n_qkv], mine[n_qkv : n_qkv + n_out], s_ffin, own[cut : cut + tall][None])
    s_gain = own[-tail:].reshape(tail * width)[:slots].reshape(gains.shape)
    s_table = lax.psum(g_table, "fsdp")
    return (
        result[None],
        dx[None],
        enc_grad[None],
        jnp.transpose(s_main[0], (1, 0, 2)),
        jnp.transpose(s_main[1], (1, 0, 2)),
        jnp.transpose(s_main[2], (1, 0, 2)),
        s_main[3][0],
        s_gain,
        s_table,
    )


def planes_of(array, number):
    width = array.shape[-1] // number
    return [array[..., at * width : (at + 1) * width] for at in range(number)]


def layer_forward(rows, enc, length, bucket_ids, weights, table):
    (w_qkv, w_qc, w_kvc), (w_o, w_oc), w_in, w_out, gains = weights
    positions = rows.shape[0]
    gain_f = gains.astype(jnp.float32)
    start = rows.astype(jnp.float32)
    h1, n1, r1 = rms_fwd(start, gain_f[0])
    qkv = planes_of(prod("ld,de->le", h1, w_qkv).astype(jnp.bfloat16), 3)
    row_ids = lax.broadcasted_iota(jnp.int32, (positions, positions), 0)
    col_ids = lax.broadcasted_iota(jnp.int32, (positions, positions), 1)
    mask = (col_ids <= row_ids) & (col_ids < length)
    bias, onehot = toeplitz_bias(bucket_ids, table, positions)
    a1, lse1 = attend(qkv[0], qkv[1], qkv[2], bias, mask, True)
    x1 = start + prod("le,ed->ld", a1, w_o)
    h2, n2, r2 = rms_fwd(x1, gain_f[1])
    qc = prod("ld,de->le", h2, w_qc).astype(jnp.bfloat16)
    kvc = planes_of(prod("ld,de->le", enc, w_kvc).astype(jnp.bfloat16), 2)
    ac, lse2 = attend(qc, kvc[0], kvc[1], None, None, False)
    x2 = x1 + prod("le,ed->ld", ac, w_oc)
    h3, n3, r3 = rms_fwd(x2, gain_f[2])
    gate_up = planes_of(prod("ld,df->lf", h3, w_in), 2)
    hidden = (gelu_tanh(gate_up[0]) * gate_up[1]).astype(jnp.bfloat16)
    result = x2 + prod("lf,fd->ld", hidden, w_out)
    saved = (h1, n1, r1, qkv, bias, mask, a1, lse1, h2, n2, r2, qc, kvc, ac, lse2, h3, n3, r3)
    return (result.astype(jnp.bfloat16), saved + (gate_up, hidden, onehot))


def layer_back(saved, weights, enc, cot):
    (w_qkv, w_qc, w_kvc), (w_o, w_oc), w_in, w_out, gains = weights
    gain_f = gains.astype(jnp.float32)
    (h1, n1, r1, qkv, bias, mask, a1, lse1, h2, n2, r2, qc, kvc, ac, lse2, h3, n3, r3) = saved[:18]
    gate_up, hidden, onehot = saved[18:]
    g_out = prod("lf,ld->fd", hidden, cot)
    d_hidden = prod("ld,fd->lf", cot, w_out)
    gelu_val, gelu_pull = jax.vjp(gelu_tanh, gate_up[0])
    d_gate = gelu_pull(d_hidden * gate_up[1])[0]
    d_gate_up = jnp.concatenate([d_gate, d_hidden * gelu_val], axis=1).astype(jnp.bfloat16)
    g_in = prod("ld,lf->df", h3, d_gate_up)
    back3, gain3 = rms_bwd(prod("lf,df->ld", d_gate_up, w_in), n3, r3, gain_f[2])
    dx2 = cot.astype(jnp.float32) + back3
    dx2_b = dx2.astype(jnp.bfloat16)
    g_oc = prod("le,ld->ed", ac, dx2_b)
    d_ac = prod("ld,ed->le", dx2_b, w_oc)
    d_qc, d_kc, d_vc, unused = attend_back(qc, kvc[0], kvc[1], ac, lse2, d_ac, None, None)
    g_qc = prod("ld,le->de", h2, d_qc)
    d_kvc = jnp.concatenate([d_kc, d_vc], axis=1)
    g_kvc = prod("ld,le->de", enc, d_kvc)
    enc_grad = prod("le,de->ld", d_kvc, w_kvc).astype(jnp.bfloat16)
    back2, gain2 = rms_bwd(prod("le,de->ld", d_qc, w_qc), n2, r2, gain_f[1])
    dx1 = dx2 + back2
    dx1_b = dx1.astype(jnp.bfloat16)
    g_o = prod("le,ld->ed", a1, dx1_b)
    d_a1 = prod("ld,ed->le", dx1_b, w_o)
    d_q, d_k, d_v, d_score = attend_back(qkv[0], qkv[1], qkv[2], a1, lse1, d_a1, bias, mask)
    d_qkv = jnp.concatenate([d_q, d_k, d_v], axis=1)
    g_qkv = prod("ld,le->de", h1, d_qkv)
    back1, gain1 = rms_bwd(prod("le,de->ld", d_qkv, w_qkv), n1, r1, gain_f[0])
    d_table = diagonal_sums(d_score, onehot)
    grads = [g_qkv, g_o, g_qc, g_kvc, g_oc, g_in, g_out]
    return ((dx1 + back1).astype(jnp.bfloat16), enc_grad, grads, (gain1, gain2, gain3), d_table)


MESH = pl.DeviceIdType.MESH
SUB = 8


def place(count):
    me = lax.axis_index("fsdp")
    core = lax.rem(me, 2)
    x = lax.rem(me // 2, 2)
    y = lax.rem(me // 4, 2)
    z = me // 8
    return me, core, x, y, z


def device(z, y, x, core):
    return ((z * 2 + y) * 2 + x) * 2 + core


def greet(peers):
    barrier = pltpu.get_barrier_semaphore()
    total = 0
    for cond, peer in peers:

        def signal(peer=peer):
            pl.semaphore_signal(barrier, inc=1, device_id=(peer,), device_id_type=MESH)

        if cond is None:
            signal()
            total = total + 1
        else:
            pl.when(cond)(signal)
            total = total + cond.astype(jnp.int32)
    pl.semaphore_wait(barrier, total)


def both(first, second):
    if first is None:
        return second
    if second is None:
        return first
    return jnp.logical_and(first, second)


class Sender:
    def __init__(self, sems):
        self.sems = sems
        self.used = 0
        self.open = []

    def start(self, src, dst, recv, target, cond=None):
        copy = pltpu.make_async_remote_copy(
            src_ref=src,
            dst_ref=dst,
            send_sem=self.sems.at[self.used],
            recv_sem=recv,
            device_id=(target,),
            device_id_type=MESH,
        )
        self.used += 1
        self.open.append((cond, copy))
        if cond is None:
            copy.start()
        else:
            pl.when(cond)(copy.start)

    def finish(self):
        for cond, copy in self.open:
            if cond is None:
                copy.wait_send()
            else:
                pl.when(cond)(copy.wait_send)


def gather_kernel(planes, groups, *refs):
    ins, outs = refs[:groups], refs[groups : 2 * groups]
    local_sem, send_sem, recv_sem = refs[2 * groups :]
    me, core, x, y, z = place(planes)
    partner, across, along = device(z, y, x, 1 - core), device(z, y, 1 - x, core), device(z, 1 - y, x, core)
    up, down = device(z + 1, y, x, core), device(z - 1, y, x, core)
    can_up, can_down = z < planes - 1, z > 0
    half = planes // 2
    greet([(None, partner), (None, across), (None, along), (can_up, up), (can_down, down)])
    sender = Sender(send_sem)

    def arrive(g, src, cond):
        copy = pltpu.make_async_remote_copy(
            src_ref=outs[g].at[src],
            dst_ref=outs[g].at[src],
            send_sem=send_sem.at[0],
            recv_sem=recv_sem.at[g, src],
            device_id=(partner,),
            device_id_type=MESH,
        )
        if cond is None:
            copy.wait_recv()
        else:
            pl.when(cond)(copy.wait_recv)

    def send(g, src, target, cond, own=False):
        sender.start(
            ins[g] if own else outs[g].at[src], outs[g].at[src], recv_sem.at[g, src], target, cond
        )

    def steps(k):
        if k == 0:
            return [(None, z)]
        return [(z - k >= 0, z - k), (z + k < planes, z + k)]

    def line(k):
        for g in range(groups):
            for side, (cond, zs) in enumerate(steps(k)):
                src = device(zs, y, x, core)
                if k:
                    arrive(g, src, cond)
                if k == 0 or side == 0:
                    send(g, src, up, both(cond, can_up), k == 0)
                if k == 0 or side == 1:
                    send(g, src, down, both(cond, can_down), k == 0)
                send(g, src, across, cond, k == 0)
                send(g, src, along, cond, k == 0)
                send(g, src, partner, cond, k == 0)

    def plane(k):
        for g in range(groups):
            for cond, zs in steps(k):
                src = device(zs, y, 1 - x, core)
                arrive(g, src, cond)
                send(g, src, along, both(cond, zs >= half))
                send(g, src, partner, cond)
                src = device(zs, 1 - y, x, core)
                arrive(g, src, cond)
                send(g, src, across, both(cond, zs < half))
                send(g, src, partner, cond)

    def corner(k):
        for g in range(groups):
            for cond, zs in steps(k):
                src = device(zs, 1 - y, 1 - x, core)
                arrive(g, src, cond)
                send(g, src, partner, cond)

    line(0)
    for g in range(groups):
        pltpu.make_async_copy(ins[g], outs[g].at[me], local_sem.at[g]).start()
    for k in range(planes):
        if k + 1 < planes:
            line(k + 1)
        plane(k)
        if k:
            corner(k - 1)
    corner(planes - 1)
    for g in range(groups):
        for zs in range(planes):
            for ys in range(2):
                for xs in range(2):
                    arrive(g, device(zs, ys, xs, 1 - core), None)
    sender.finish()
    for g in range(groups):
        pltpu.make_async_copy(ins[g], outs[g].at[me], local_sem.at[g]).wait()


def gather(shards, count):
    planes, groups = count // 8, len(shards)
    sites = groups * (5 + (planes - 1) * 8 + (2 * planes - 1) * 5)
    spec = pl.BlockSpec(memory_space=pl.ANY)
    return pl.pallas_call(
        functools.partial(gather_kernel, planes, groups),
        out_shape=tuple(jax.ShapeDtypeStruct((count,) + s.shape, s.dtype) for s in shards),
        in_specs=[spec] * groups,
        out_specs=tuple([spec] * groups),
        scratch_shapes=[
            pltpu.SemaphoreType.DMA((groups,)),
            pltpu.SemaphoreType.DMA((sites,)),
            pltpu.SemaphoreType.DMA((groups, count)),
        ],
        compiler_params=pltpu.CompilerParams(collective_id=0, has_side_effects=True),
        name="gather",
    )(*shards)


def scatter_kernel(planes, groups, *refs):
    grads, small = refs[:groups], refs[groups]
    outs, small_out = refs[groups + 1 : 2 * groups + 1], refs[2 * groups + 1]
    rest = refs[2 * groups + 2 :]
    mine, theirs, from_x, from_y, line_x, line_y, line_u, line_d = (
        rest[i * groups : (i + 1) * groups] for i in range(8)
    )
    held, got, local_sem, send_sem, pair_sem, half_sem, line_sem, chain_sem, small_sem = rest[8 * groups :]
    me, core, x, y, z = place(planes)
    partner, across, along = device(z, y, x, 1 - core), device(z, y, 1 - x, core), device(z, 1 - y, x, core)
    up, down = device(z + 1, y, x, core), device(z - 1, y, x, core)
    can_up, can_down = z < planes - 1, z > 0
    half = planes // 2
    others = [device(lax.rem(z + k, planes), y, x, core) for k in range(1, planes)]
    greet([(None, p) for p in (partner, across, along, *others)])
    sender = Sender(send_sem)

    def wait(dst, sem, cond=None):
        copy = pltpu.make_async_remote_copy(
            src_ref=dst,
            dst_ref=dst,
            send_sem=send_sem.at[0],
            recv_sem=sem,
            device_id=(partner,),
            device_id_type=MESH,
        )
        if cond is None:
            copy.wait_recv()
        else:
            pl.when(cond)(copy.wait_recv)

    lines = [(1 - y, 1 - x), (y, 1 - x), (1 - y, x), (y, x)]

    def local(g):
        return pltpu.make_async_copy(grads[g].at[:, :, :, core], mine[g], local_sem.at[g])

    for g in range(groups):
        local(g).start()
    for at, (ys, xs) in enumerate(lines):
        for g in range(groups):
            sender.start(
                grads[g].at[:, ys, xs, 1 - core], theirs[g].at[:, ys, xs], pair_sem.at[g, at], partner
            )

    def add(g, ys, xs, low, high, terms):
        depth = mine[g].shape[3]

        def body(i, carry):
            zs, r = low + i // depth, lax.rem(i, depth)
            total = mine[g][zs, ys, xs, r].astype(jnp.float32)
            for term in terms:
                total = total + term(zs, r).astype(jnp.float32)
            mine[g][zs, ys, xs, r] = total.astype(jnp.bfloat16)
            return carry

        lax.fori_loop(0, (high - low) * depth, body, 0)

    def pair(g, ys, xs):
        return lambda zs, r: theirs[g][zs, ys, xs, r]

    held[0] = small[...]
    for r, peer in enumerate((partner, across, along)):
        sender.start(held.at[r], got.at[r], small_sem.at[r], peer)

        wait(got.at[r], small_sem.at[r])
        held[r + 1] = held[r] + got[r]
    for peer in others:
        sender.start(held.at[3], got.at[3 + z], small_sem.at[3 + z], peer)

    ys, xs = lines[0]
    for g in range(groups):
        local(g).wait()
        wait(theirs[g].at[:, ys, xs], pair_sem.at[g, 0])
        add(g, ys, xs, 0, half, [pair(g, ys, xs)])
        sender.start(mine[g].at[pl.ds(0, half), ys, xs], from_x[g], half_sem.at[g, 0], across)
        add(g, ys, xs, half, planes, [pair(g, ys, xs)])
        sender.start(
            mine[g].at[pl.ds(half, planes - half), ys, xs], from_y[g], half_sem.at[g, 1], along
        )
    low, high = pl.ds(0, half), pl.ds(half, planes - half)
    for g in range(groups):
        ys, xs = lines[1]
        wait(theirs[g].at[:, ys, xs], pair_sem.at[g, 1])
        add(g, ys, xs, 0, half, [pair(g, ys, xs)])
        sender.start(mine[g].at[low, ys, xs], line_x[g].at[low], line_sem.at[g, 0], across)
        ys, xs = lines[2]
        wait(theirs[g].at[:, ys, xs], pair_sem.at[g, 2])
        add(g, ys, xs, half, planes, [pair(g, ys, xs)])
        sender.start(mine[g].at[high, ys, xs], line_y[g].at[high], line_sem.at[g, 3], along)
    for g in range(groups):
        ys, xs = lines[1]
        wait(from_y[g], half_sem.at[g, 1])
        add(g, ys, xs, half, planes, [pair(g, ys, xs), lambda zs, r, g=g: from_y[g][zs - half, r]])
        sender.start(mine[g].at[high, ys, xs], line_x[g].at[high], line_sem.at[g, 1], across)
        ys, xs = lines[2]
        wait(from_x[g], half_sem.at[g, 0])
        add(g, ys, xs, 0, half, [pair(g, ys, xs), lambda zs, r, g=g: from_x[g][zs, r]])
        sender.start(mine[g].at[low, ys, xs], line_y[g].at[low], line_sem.at[g, 2], along)
    for g in range(groups):
        wait(theirs[g].at[:, y, x], pair_sem.at[g, 3])
        wait(line_x[g].at[low], line_sem.at[g, 0])
        wait(line_x[g].at[high], line_sem.at[g, 1])
        wait(line_y[g].at[low], line_sem.at[g, 2])
        wait(line_y[g].at[high], line_sem.at[g, 3])
        add(
            g, y, x, 0, planes,
            [pair(g, y, x), lambda zs, r, g=g: line_x[g][zs, r], lambda zs, r, g=g: line_y[g][zs, r]],
        )
        for k in range(planes - 1, 0, -1):
            chain(g, k, wait, sender, mine, (line_u, line_d), chain_sem, (y, x, z, planes), (up, down))
    for g in range(groups):
        wait(line_u[g].at[z], chain_sem.at[g, 0, z], can_down)
        wait(line_d[g].at[z], chain_sem.at[g, 1, z], can_up)
        depth = mine[g].shape[3]
        zero = jnp.zeros(mine[g].shape[4:], jnp.float32)

        def body(r, carry, g=g):
            total = mine[g][z, y, x, r].astype(jnp.float32)
            total = total + jnp.where(can_down, line_u[g][z, r].astype(jnp.float32), zero)
            total = total + jnp.where(can_up, line_d[g][z, r].astype(jnp.float32), zero)
            outs[g][r] = total
            return carry

        lax.fori_loop(0, depth, body, 0)
    for k in range(1, planes):
        at = lax.rem(z + k, planes)
        wait(got.at[3 + at], small_sem.at[3 + at])
    got[3 + z] = held[3]
    total = got[3]
    for zs in range(1, planes):
        total = total + got[3 + zs]
    small_out[...] = total
    sender.finish()


def chain(g, k, wait, sender, mine, lines, sems, where, targets):
    y, x, z, planes = where
    for way, (at, inside, fed) in enumerate(
        ((z + k, z + k < planes, z > 0), (z - k, z - k >= 0, z < planes - 1))
    ):
        spot = jnp.clip(at, 0, planes - 1)
        join = both(inside, fed)

        @pl.when(join)
        def _(way=way, spot=spot):
            wait(lines[way][g].at[spot], sems.at[g, way, spot])
            depth = mine[g].shape[3]

            def body(r, carry):
                total = mine[g][spot, y, x, r].astype(jnp.float32) + lines[way][g][spot, r].astype(jnp.float32)
                mine[g][spot, y, x, r] = total.astype(jnp.bfloat16)
                return carry

            lax.fori_loop(0, depth, body, 0)

        sender.start(mine[g].at[spot, y, x], lines[way][g].at[spot], sems.at[g, way, spot], targets[way], inside)


def scatter(grads, small, count):
    planes, groups = count // 8, len(grads)
    half = planes // 2
    blocks = [g.shape[4:] for g in grads]
    any_spec, vmem = pl.BlockSpec(memory_space=pl.ANY), pl.BlockSpec(memory_space=pltpu.VMEM)
    sites = groups * (4 + 2 + 4 + 2 * (planes - 1)) + 3 + planes

    def room(*lead):
        return [pltpu.VMEM(lead + b, jnp.bfloat16) for b in blocks]

    return pl.pallas_call(
        functools.partial(scatter_kernel, planes, groups),
        out_shape=tuple(jax.ShapeDtypeStruct(b, jnp.float32) for b in blocks)
        + (jax.ShapeDtypeStruct(small.shape, jnp.float32),),
        in_specs=[any_spec] * groups + [vmem],
        out_specs=tuple([vmem] * (groups + 1)),
        scratch_shapes=room(planes, 2, 2)
        + room(planes, 2, 2)
        + room(half)
        + room(planes - half)
        + room(planes) * 1
        + room(planes)
        + room(planes)
        + room(planes)
        + [
            pltpu.VMEM((4,) + small.shape, jnp.float32),
            pltpu.VMEM((3 + planes,) + small.shape, jnp.float32),
            pltpu.SemaphoreType.DMA((groups,)),
            pltpu.SemaphoreType.DMA((sites,)),
            pltpu.SemaphoreType.DMA((groups, 4)),
            pltpu.SemaphoreType.DMA((groups, 2)),
            pltpu.SemaphoreType.DMA((groups, 4)),
            pltpu.SemaphoreType.DMA((groups, 2, planes)),
            pltpu.SemaphoreType.DMA((3 + planes,)),
        ],
        compiler_params=pltpu.CompilerParams(
            collective_id=1, has_side_effects=True, vmem_limit_bytes=60 * 1024 * 1024
        ),
        name="scatter",
    )(*grads, small)


def per_device(
    inputs, encoded, lengths, bucket_ids, qkv_weights, out_weights, ff_in, ff_out, gains, bias_table, cotangent
):
    count = lax.axis_size("fsdp")
    me = lax.axis_index("fsdp")
    depth, width, hidden = qkv_weights.shape[0], qkv_weights.shape[-1], ff_in.shape[-1]
    tall = ff_out.shape[0]
    pairs = [
        qkv_weights[:, 0:3].reshape(depth, 3 * width),
        out_weights[:, 0],
        qkv_weights[:, 3],
        qkv_weights[:, 4:6].reshape(depth, 2 * width),
        out_weights[:, 1],
        ff_in.reshape(depth, 2 * hidden),
        ff_out,
    ]
    gain_row = lax.dynamic_update_slice(
        jnp.zeros((SUB, width), jnp.bfloat16), gains, (jnp.int32(0), me * gains.shape[1])
    )
    shards = [gain_row] + pairs
    shards = [s.reshape(-1, SUB, s.shape[-1]) for s in shards]
    got = gather(shards, count)
    gain_all = jnp.sum(got[0].astype(jnp.float32), axis=(0, 1))[: gains.shape[0]].astype(jnp.bfloat16)
    w_qkv, w_o, w_qc, w_kvc, w_oc, w_in, w_out = (w.reshape(-1, w.shape[-1]) for w in got[1:])

    qkv_w = [w_qkv, w_qc, w_kvc]
    weights = (qkv_w, (w_o, w_oc), w_in, w_out, gain_all)
    result, saved = layer_forward(inputs[0], encoded[0], lengths[0], bucket_ids, weights, bias_table)
    dx, enc_grad, grads, (gain1, gain2, gain3), g_table = layer_back(
        saved, weights, encoded[0], cotangent[0]
    )
    planes = count // 8
    parts = [
        g.astype(jnp.bfloat16).reshape(planes, 2, 2, 2, -1, SUB, g.shape[-1]) for g in grads
    ]
    lanes = 128
    flat = jnp.concatenate([jnp.stack([gain1, gain2, gain3]).reshape(-1), g_table.reshape(-1)])
    rows = SUB * -(-flat.size // (SUB * lanes))
    small = jnp.pad(flat, (0, rows * lanes - flat.size)).reshape(rows, lanes)
    own = scatter(parts, small, count)
    total = own[-1].reshape(-1)
    o_qkv, o_o, o_qc, o_kvc, o_oc, o_in, o_out = (o.reshape(-1, o.shape[-1]) for o in own[:-1])
    s_gain = total[: gains.shape[0] * width].reshape(gains.shape[0], width)
    s_gain = lax.dynamic_slice(s_gain, (jnp.int32(0), me * gains.shape[1]), gains.shape)
    s_table = total[gains.shape[0] * width : flat.size].reshape(bias_table.shape)
    return (
        result[None],
        dx[None],
        enc_grad[None],
        jnp.concatenate([o_qkv, o_qc, o_kvc], axis=1).reshape(qkv_weights.shape),
        jnp.concatenate([o_o, o_oc], axis=1).reshape(out_weights.shape),
        o_in.reshape(ff_in.shape),
        o_out,
        s_gain,
        s_table,
    )


def solution(mesh):
    count = mesh.shape["fsdp"]

    def layer(*args):
        depth, tall = args[4].shape[0], args[7].shape[0]
        tiled = depth % SUB == 0 and tall % SUB == 0 and count % 8 == 0 and count > 8
        return (per_device if tiled else plain_device)(*args)

    rows, split = P("fsdp", None, None), P("fsdp", None)
    return jax.shard_map(
        layer,
        mesh=mesh,
        in_specs=(rows, rows, P("fsdp"), P(), rows, rows, rows, split, P(None, "fsdp"), P(), rows),
        out_specs=(rows, rows, rows, rows, rows, rows, split, P(None, "fsdp"), P()),
        check_vma=False,
    )
```

```python
import types

import jax
import jax.numpy as jnp
from jax import lax
from jax.experimental import pallas as pl
from jax.experimental.pallas import tpu as pltpu
from jax.sharding import PartitionSpec as P

HEAD = 64


EPS = 1e-06


def prod(form, left, right):
    return jnp.einsum(form, left, right, preferred_element_type=jnp.float32)


def gelu_tanh(value):
    return (
        0.5
        * value
        * (1.0 + jnp.tanh(0.7978845608028654 * (value + 0.044715 * value * value * value)))
    )


def rms_fwd(value, gain):
    recip = lax.rsqrt(jnp.mean(value * value, axis=-1, keepdims=True) + EPS)
    normed = value * recip
    return ((normed * gain).astype(jnp.bfloat16), normed, recip)


def rms_bwd(grad, normed, recip, gain):
    scaled = grad * gain
    gain_grad = jnp.sum(grad * normed, axis=0)
    back = recip * (scaled - normed * jnp.mean(scaled * normed, axis=-1, keepdims=True))
    return (back, gain_grad)


def toeplitz_bias(bucket_ids, table, positions):
    onehot = (bucket_ids[:, None] == jnp.arange(table.shape[0], dtype=jnp.int32)[None, :]).astype(
        jnp.float32
    )
    by_dist = jnp.transpose(jnp.dot(onehot, table, precision=lax.Precision.HIGHEST), (1, 0))
    head_count = by_dist.shape[0]
    nearest = jnp.broadcast_to(by_dist[:, 0:1], (head_count, positions))
    cyclic = jnp.concatenate(
        [nearest, jnp.zeros((head_count, 1), jnp.float32), by_dist[:, :0:-1]], axis=1
    )
    tiled = jnp.broadcast_to(cyclic[:, None, :], (head_count, positions, 2 * positions))
    tiled = tiled.reshape(head_count, 2 * positions * positions)
    skewed = tiled[:, : positions * (2 * positions - 1)].reshape(
        head_count, positions, 2 * positions - 1
    )
    return (skewed[:, :, :positions], onehot)


def diagonal_sums(d_score, onehot):
    head_count, positions = (d_score.shape[0], d_score.shape[1])
    padded = jnp.pad(d_score, ((0, 0), (0, 0), (0, positions - 1)))
    padded = padded.reshape(head_count, positions * (2 * positions - 1))
    padded = jnp.pad(padded, ((0, 0), (0, positions))).reshape(head_count, positions, 2 * positions)
    column = jnp.sum(padded, axis=1)
    by_dist = jnp.concatenate(
        [jnp.sum(column[:, :positions], axis=1, keepdims=True), column[:, :positions:-1]], axis=1
    )
    return jnp.dot(
        jnp.transpose(onehot, (1, 0)),
        jnp.transpose(by_dist, (1, 0)),
        precision=lax.Precision.HIGHEST,
    )


def scores_of(query, keys, bias, mask):
    rows = query.shape[0]
    q3 = query.reshape(rows, -1, HEAD)
    k3 = keys.reshape(keys.shape[0], -1, HEAD)
    scores = prod("qhd,khd->hqk", q3, k3)
    if bias is not None:
        scores = scores + bias
    if mask is not None:
        scores = jnp.where(mask[None], scores, -1e30)
    return scores


def attend(query, keys, values, bias, mask, shifted):
    rows = query.shape[0]
    scores = scores_of(query, keys, bias, mask)
    if shifted:
        top = jnp.max(scores, axis=-1, keepdims=True)
        lse = top + jnp.log(jnp.sum(jnp.exp(scores - top), axis=-1, keepdims=True))
    else:
        lse = jnp.log(jnp.sum(jnp.exp(scores), axis=-1, keepdims=True))
    prob = jnp.exp(scores - lse).astype(jnp.bfloat16)
    v3 = values.reshape(values.shape[0], -1, HEAD)
    out = prod("hqk,khd->qhd", prob, v3).reshape(rows, -1).astype(jnp.bfloat16)
    return (out, lse)


def attend_back(query, keys, values, out, lse, grad_out, bias, mask):
    rows = query.shape[0]
    scores = scores_of(query, keys, bias, mask)
    prob = jnp.exp(scores - lse)
    prob_b = prob.astype(jnp.bfloat16)
    q3 = query.reshape(rows, -1, HEAD)
    k3 = keys.reshape(keys.shape[0], -1, HEAD)
    v3 = values.reshape(values.shape[0], -1, HEAD)
    grad3 = grad_out.reshape(rows, -1, HEAD)
    grad_b = grad3.astype(jnp.bfloat16)
    out3 = out.reshape(rows, -1, HEAD).astype(jnp.float32)
    d_val = prod("hqk,qhd->khd", prob_b, grad_b)
    d_prob = prod("qhd,khd->hqk", grad_b, v3)
    delta = jnp.transpose(jnp.sum(grad3 * out3, axis=2), (1, 0))
    d_score = prob * (d_prob - delta[:, :, None])
    d_score_b = d_score.astype(jnp.bfloat16)
    d_query = prod("hqk,khd->qhd", d_score_b, k3)
    d_key = prod("hqk,qhd->khd", d_score_b, q3)
    shape_q = (rows, -1)
    shape_k = (keys.shape[0], -1)
    return (
        d_query.reshape(shape_q).astype(jnp.bfloat16),
        d_key.reshape(shape_k).astype(jnp.bfloat16),
        d_val.reshape(shape_k).astype(jnp.bfloat16),
        d_score,
    )


def forward(rows, enc, length, bucket_ids, weights, table):
    qkv_w, out_w, ff_in, ff_out, gains = weights
    positions = rows.shape[0]
    gain_f = gains.astype(jnp.float32)
    start = rows.astype(jnp.float32)
    h1, n1, r1 = rms_fwd(start, gain_f[0])
    qkv = prod("ld,cde->cle", h1, qkv_w[0:3]).astype(jnp.bfloat16)
    row_ids = lax.broadcasted_iota(jnp.int32, (positions, positions), 0)
    col_ids = lax.broadcasted_iota(jnp.int32, (positions, positions), 1)
    mask = (col_ids <= row_ids) & (col_ids < length)
    bias, onehot = toeplitz_bias(bucket_ids, table, positions)
    a1, lse1 = attend(qkv[0], qkv[1], qkv[2], bias, mask, True)
    x1 = start + prod("le,ed->ld", a1, out_w[0])
    h2, n2, r2 = rms_fwd(x1, gain_f[1])
    qc = prod("ld,de->le", h2, qkv_w[3]).astype(jnp.bfloat16)
    kvc = prod("ld,cde->cle", enc, qkv_w[4:6]).astype(jnp.bfloat16)
    ac, lse2 = attend(qc, kvc[0], kvc[1], None, None, False)
    x2 = x1 + prod("le,ed->ld", ac, out_w[1])
    h3, n3, r3 = rms_fwd(x2, gain_f[2])
    gate_up = prod("ld,cdf->clf", h3, ff_in)
    hidden = (gelu_tanh(gate_up[0]) * gate_up[1]).astype(jnp.bfloat16)
    result = x2 + prod("lf,fd->ld", hidden, ff_out)
    saved = (
        h1,
        n1,
        r1,
        qkv,
        bias,
        mask,
        a1,
        lse1,
        h2,
        n2,
        r2,
        qc,
        kvc,
        ac,
        lse2,
        h3,
        n3,
        r3,
        gate_up,
        hidden,
        onehot,
    )
    return (result.astype(jnp.bfloat16), saved)


def ff_back(saved, weights, cot):
    qkv_w, out_w, ff_in, ff_out, gains = weights
    gain_f = gains.astype(jnp.float32)
    h3, n3, r3, gate_up, hidden = (saved[15], saved[16], saved[17], saved[18], saved[19])
    d_ffout = prod("lf,ld->fd", hidden, cot)
    d_hidden = prod("ld,fd->lf", cot, ff_out)
    gelu_val, gelu_pull = jax.vjp(gelu_tanh, gate_up[0])
    d_gate = gelu_pull(d_hidden * gate_up[1])[0]
    d_up = d_hidden * gelu_val
    d_gate_up = jnp.stack([d_gate, d_up]).astype(jnp.bfloat16)
    d_ffin = prod("ld,clf->cdf", h3, d_gate_up)
    d_h3 = prod("clf,cdf->ld", d_gate_up, ff_in)
    back3, gain3 = rms_bwd(d_h3, n3, r3, gain_f[2])
    return (cot.astype(jnp.float32) + back3, d_ffin, d_ffout, gain3)


def cross_back(saved, weights, enc, dx2):
    qkv_w, out_w, ff_in, ff_out, gains = weights
    gain_f = gains.astype(jnp.float32)
    h2, n2, r2, qc, kvc, ac, lse2 = (
        saved[8],
        saved[9],
        saved[10],
        saved[11],
        saved[12],
        saved[13],
        saved[14],
    )
    dx2_b = dx2.astype(jnp.bfloat16)
    d_outc = prod("le,ld->ed", ac, dx2_b)
    d_ac = prod("ld,ed->le", dx2_b, out_w[1])
    d_qc, d_kc, d_vc, unused = attend_back(qc, kvc[0], kvc[1], ac, lse2, d_ac, None, None)
    g_qc = prod("ld,le->de", h2, d_qc)
    d_kvc = jnp.stack([d_kc, d_vc])
    g_kvc = prod("ld,cle->cde", enc, d_kvc)
    enc_grad = prod("cle,cde->ld", d_kvc, qkv_w[4:6]).astype(jnp.bfloat16)
    d_h2 = prod("le,de->ld", d_qc, qkv_w[3])
    back2, gain2 = rms_bwd(d_h2, n2, r2, gain_f[1])
    return (dx2 + back2, g_qc, g_kvc, d_outc, gain2, enc_grad)


def self_back(saved, weights, dx1):
    qkv_w, out_w, ff_in, ff_out, gains = weights
    gain_f = gains.astype(jnp.float32)
    h1, n1, r1, qkv, bias, mask, a1, lse1 = saved[0:8]
    onehot = saved[20]
    dx1_b = dx1.astype(jnp.bfloat16)
    d_outs = prod("le,ld->ed", a1, dx1_b)
    d_a1 = prod("ld,ed->le", dx1_b, out_w[0])
    d_q, d_k, d_v, d_score = attend_back(qkv[0], qkv[1], qkv[2], a1, lse1, d_a1, bias, mask)
    d_qkv = jnp.stack([d_q, d_k, d_v])
    g_qkv = prod("ld,cle->cde", h1, d_qkv)
    d_h1 = prod("cle,cde->ld", d_qkv, qkv_w[0:3])
    back1, gain1 = rms_bwd(d_h1, n1, r1, gain_f[0])
    d_table = diagonal_sums(d_score, onehot)
    return ((dx1 + back1).astype(jnp.bfloat16), g_qkv, d_outs, gain1, d_table)


def to_blocks(array, width):
    blocks = []
    for copy in range(array.shape[0]):
        for start in range(0, array.shape[-1], width):
            block = array[copy, ..., start : start + width]
            short = width - block.shape[-1]
            if short:
                block = jnp.pad(block, ((0, 0),) * (block.ndim - 1) + ((0, short),))
            blocks.append(block)
    return blocks


def from_blocks(blocks, shape, width):
    copies, rows, columns = shape
    each = -(-columns // width)
    planes = []
    for copy in range(copies):
        part = [blocks[copy * each + at] for at in range(each)]
        part[-1] = part[-1][..., : columns - (each - 1) * width]
        planes.append(part[0] if each == 1 else jnp.concatenate(part, axis=-1))
    return planes


def plain_device(
    inputs,
    encoded,
    lengths,
    bucket_ids,
    qkv_weights,
    out_weights,
    ff_in,
    ff_out,
    gains,
    bias_table,
    cotangent,
):
    count = lax.axis_size("fsdp")
    shards = (
        jnp.transpose(qkv_weights, (1, 0, 2)),
        jnp.transpose(out_weights, (1, 0, 2)),
        jnp.transpose(ff_in, (1, 0, 2)),
        ff_out[None],
    )
    width = qkv_weights.shape[-1]
    depth = qkv_weights.shape[0]
    tall = ff_out.shape[0]
    blocks = to_blocks(shards[0], width) + to_blocks(shards[1], width) + to_blocks(shards[2], width)
    slots = gains.size
    tail = 8 * -(-slots // (8 * width))
    gain_rows = jnp.pad(gains.reshape(1, slots), ((0, 0), (0, tail * width - slots)))
    packed = jnp.concatenate(blocks + [ff_out, gain_rows.reshape(tail, width)], axis=0)
    whole = lax.all_gather(packed, "fsdp", axis=0, tiled=False)
    cut = len(blocks) * depth
    stacked = whole[:, :cut].reshape(count, len(blocks), depth, width)
    stacked = jnp.transpose(stacked, (1, 0, 2, 3)).reshape(len(blocks), count * depth, width)
    ff_out_all = whole[:, cut : cut + tall].reshape(count * tall, width)
    stacked, ff_out_all = lax.optimization_barrier((stacked, ff_out_all))
    n_qkv, n_out = qkv_weights.shape[1], out_weights.shape[1]
    ff_all = jnp.stack(from_blocks(stacked[n_qkv + n_out :], shards[2].shape, width))
    main = (stacked[:n_qkv], stacked[n_qkv : n_qkv + n_out], ff_all, ff_out_all[None])
    gain_all = whole[:, -tail:].reshape(count, tail * width)[:, :slots]
    gain_all = gain_all.reshape(count, gains.shape[0], gains.shape[1])
    gain_all = jnp.transpose(gain_all, (1, 0, 2)).reshape(gains.shape[0], -1)
    weights = (main[0], main[1], main[2], main[3][0], gain_all)
    result, saved = forward(inputs[0], encoded[0], lengths[0], bucket_ids, weights, bias_table)
    dx2, g_ffin, g_ffout, gain3 = ff_back(saved, weights, cotangent[0])
    dx1, g_qc, g_kvc, g_outc, gain2, enc_grad = cross_back(saved, weights, encoded[0], dx2)
    dx, g_qkvs, g_outs, gain1, g_table = self_back(saved, weights, dx1)
    wide = [g_qkvs[0], g_qkvs[1], g_qkvs[2], g_qc, g_kvc[0], g_kvc[1], g_outs, g_outc]
    wide += to_blocks(g_ffin, width)
    wide.append(g_ffout)
    g_gain = jnp.stack([gain1, gain2, gain3]).reshape(gains.shape[0], count, -1)
    g_gain = jnp.transpose(g_gain, (1, 0, 2)).reshape(count, slots)
    g_gain = jnp.pad(g_gain, ((0, 0), (0, tail * width - slots))).reshape(count, tail, width)
    parts = [grad.astype(jnp.bfloat16).reshape(count, -1, width) for grad in wide]
    send = jnp.concatenate(parts + [g_gain.astype(jnp.bfloat16)], axis=1)
    send, g_table = lax.optimization_barrier((send, g_table))
    own = lax.psum_scatter(send, "fsdp", scatter_dimension=0, tiled=False).astype(jnp.float32)
    mine = own[:cut].reshape(len(blocks), depth, width)
    s_ffin = jnp.stack(from_blocks(mine[n_qkv + n_out :], shards[2].shape, width))
    s_main = (mine[:n_qkv], mine[n_qkv : n_qkv + n_out], s_ffin, own[cut : cut + tall][None])
    s_gain = own[-tail:].reshape(tail * width)[:slots].reshape(gains.shape)
    s_table = lax.psum(g_table, "fsdp")
    return (
        result[None],
        dx[None],
        enc_grad[None],
        jnp.transpose(s_main[0], (1, 0, 2)),
        jnp.transpose(s_main[1], (1, 0, 2)),
        jnp.transpose(s_main[2], (1, 0, 2)),
        s_main[3][0],
        s_gain,
        s_table,
    )


MESH = pl.DeviceIdType.MESH
SUB, LANES, TILE = 8, 128, 256
GAIN, QKV, OUT, QC, KVC, OUTC, FFIN, FFOUT = range(8)
NT = (((1,), (1,)), ((), ()))
TN = (((0,), (0,)), ((), ()))
NN = (((1,), (0,)), ((), ()))


def dot(left, right, dims=NN):
    return lax.dot_general(left, right, dims, preferred_element_type=jnp.float32)


def place():
    me = lax.axis_index("fsdp")
    return me, lax.rem(me, 2), lax.rem(me // 2, 2), lax.rem(me // 4, 2), me // 8


def device(z, y, x, core):
    return ((z * 2 + y) * 2 + x) * 2 + core


def both(first, second):
    if first is None:
        return second
    if second is None:
        return first
    return jnp.logical_and(first, second)


def maybe(cond, action):
    if cond is None:
        action()
    else:
        pl.when(cond)(action)


class Sender:
    def __init__(self, sems, anyone):
        self.sems = sems
        self.anyone = anyone
        self.used = 0
        self.open = []

    def start(self, src, dst, recv, target, cond=None):
        copy = pltpu.make_async_remote_copy(
            src_ref=src,
            dst_ref=dst,
            send_sem=self.sems.at[self.used],
            recv_sem=recv,
            device_id=(target,),
            device_id_type=MESH,
        )
        self.used += 1
        self.open.append((cond, copy))
        maybe(cond, copy.start)

    def wait(self, dst, sem, cond=None):
        copy = pltpu.make_async_remote_copy(
            src_ref=dst,
            dst_ref=dst,
            send_sem=self.sems.at[0],
            recv_sem=sem,
            device_id=(self.anyone,),
            device_id_type=MESH,
        )
        maybe(cond, copy.wait_recv)

    def finish(self):
        for cond, copy in self.open:
            maybe(cond, copy.wait_send)


def chunks(total, body):
    def step(i, carry):
        body(i, pl.ds(pl.multiple_of(i * TILE, TILE), TILE))
        return carry

    lax.fori_loop(0, total // TILE, step, 0)


def rms_parts(value):
    recip = lax.rsqrt(jnp.mean(value * value, axis=-1, keepdims=True) + EPS)
    return value * recip, recip


def gelu_and_slope(value):
    inner = 0.7978845608028654 * (value + 0.044715 * value * value * value)
    bent = jnp.tanh(inner)
    slope = 0.5 * (1.0 + bent) + 0.5 * value * (1.0 - bent * bent) * (
        0.7978845608028654 * (1.0 + 3.0 * 0.044715 * value * value)
    )
    return 0.5 * value * (1.0 + bent), slope


def layer_kernel(planes, tree, *refs):
    r = types.SimpleNamespace(**jax.tree.unflatten(tree, refs))
    me, core, x, y, z = place()
    partner, across, along = device(z, y, x, 1 - core), device(z, y, 1 - x, core), device(z, 1 - y, x, core)
    up, down = device(z + 1, y, x, core), device(z - 1, y, x, core)
    can_up, can_down = z < planes - 1, z > 0
    half = planes // 2
    others = [device(lax.rem(z + k, planes), y, x, core) for k in range(1, planes)]
    whole, shard = r.whole, r.shard
    local_sem, recv_sem, pair_sem = r.local_sem, r.recv_sem, r.pair_sem
    sender = Sender(r.send_sem, partner)

    def load_own(g):
        return pltpu.make_async_copy(shard[g], whole[g].at[me], local_sem.at[g])

    for g in range(8):
        load_own(g).start()
    barrier = pltpu.get_barrier_semaphore()
    peers = [partner, across, along, *others]
    for peer in peers:
        pl.semaphore_signal(barrier, inc=1, device_id=(peer,), device_id_type=MESH)
    pl.semaphore_wait(barrier, len(peers))

    def send(g, src, target, cond, own=False):
        sender.start(
            shard[g] if own else whole[g].at[src], whole[g].at[src], recv_sem.at[g, src], target, cond
        )

    def arrive(g, src, cond=None):
        sender.wait(whole[g].at[src], recv_sem.at[g, src], cond)

    def steps(k):
        if k == 0:
            return [(None, z)]
        return [(z - k >= 0, z - k), (z + k < planes, z + k)]

    def line(g, k):
        for side, (cond, zs) in enumerate(steps(k)):
            src = device(zs, y, x, core)
            if k:
                arrive(g, src, cond)
            if k == 0 or side == 0:
                send(g, src, up, both(cond, can_up), k == 0)
            if k == 0 or side == 1:
                send(g, src, down, both(cond, can_down), k == 0)
            send(g, src, across, cond, k == 0)
            send(g, src, along, cond, k == 0)
            send(g, src, partner, cond, k == 0)

    def plane(g, k):
        for cond, zs in steps(k):
            src = device(zs, y, 1 - x, core)
            arrive(g, src, cond)
            send(g, src, along, both(cond, zs >= half))
            send(g, src, partner, cond)
            src = device(zs, 1 - y, x, core)
            arrive(g, src, cond)
            send(g, src, across, both(cond, zs < half))
            send(g, src, partner, cond)

    def corner(g, k):
        for cond, zs in steps(k):
            src = device(zs, 1 - y, 1 - x, core)
            arrive(g, src, cond)
            send(g, src, partner, cond)

    def gather_stage(g, t):
        if t < planes:
            line(g, t)
        if 0 <= t - 1 < planes:
            plane(g, t - 1)
        if 0 <= t - 2 < planes:
            corner(g, t - 2)

    def settle(g):
        for zs in range(planes):
            for ys in range(2):
                for xs in range(2):
                    arrive(g, device(zs, ys, xs, 1 - core))
        load_own(g).wait()

    rows_t, rows_p, step_p, mine = ([None] + list(a) for a in (r.turned, r.turned_p, r.step_p, r.mine))
    step = [None] + list(r.step) + [r.cot]

    def turn(g, value):
        shape = rows_t[g].shape
        turned = jnp.transpose(value, (1, 0)).reshape((shape[1], 2) + shape[2:]).astype(jnp.bfloat16)
        rows_t[g][0] = turned[:, 0]
        rows_t[g][1] = turned[:, 1]

    def send_rows(g):
        sender.start(rows_t[g].at[1 - core], rows_p[g], pair_sem.at[g, 0], partner)

    def send_step(g):
        sender.start(step[g], step_p[g], pair_sem.at[g, 1], partner)

    def weight_grad(g):
        sender.wait(rows_p[g], pair_sem.at[g, 0])
        sender.wait(step_p[g], pair_sem.at[g, 1])
        tokens = rows_t[g].shape[-1]

        def body(i, col):
            left, left_p = rows_t[g][core].reshape(-1, tokens), rows_p[g][...].reshape(-1, tokens)
            right, right_p = step[g][:, col], step_p[g][:, col]
            if tokens % LANES == 0:
                total = dot(
                    jnp.concatenate([left, left_p], axis=1), jnp.concatenate([right, right_p], axis=0)
                )
            else:
                total = dot(left, right) + dot(left_p, right_p)
            mine[g][..., col] = total.reshape(mine[g].shape[:-1] + (TILE,)).astype(jnp.bfloat16)

        chunks(mine[g].shape[-1], body)

    from_x, from_y, line_x, line_y, line_u, line_d, own = (
        [None] + list(a) for a in (r.from_x, r.from_y, r.line_x, r.line_y, r.line_u, r.line_d, r.own)
    )
    lines = (line_u, line_d)
    half_sem, line_sem, chain_sem = r.half_sem, r.line_sem, r.chain_sem
    low, high = pl.ds(0, half), pl.ds(half, planes - half)

    def add(g, ys, xs, first, last, terms):
        depth = mine[g].shape[3]

        def body(i, carry):
            zs, at = first + i // depth, lax.rem(i, depth)
            total = mine[g][zs, ys, xs, at].astype(jnp.float32)
            for term, skip in terms:
                total = total + term[zs - skip, at].astype(jnp.float32)
            mine[g][zs, ys, xs, at] = total.astype(jnp.bfloat16)
            return carry

        lax.fori_loop(0, (last - first) * depth, body, 0)

    def scatter_stage(g, t):
        if t == 0:
            far = (1 - y, 1 - x)
            sender.start(mine[g].at[(low,) + far], from_x[g], half_sem.at[g, 0], across)
            sender.start(mine[g].at[(high,) + far], from_y[g], half_sem.at[g, 1], along)
            sender.start(mine[g].at[low, y, 1 - x], line_x[g].at[low], line_sem.at[g, 0], across)
            sender.start(mine[g].at[high, 1 - y, x], line_y[g].at[high], line_sem.at[g, 3], along)
        elif t == 1:
            sender.wait(from_y[g], half_sem.at[g, 1])
            add(g, y, 1 - x, half, planes, [(from_y[g], half)])
            sender.start(mine[g].at[high, y, 1 - x], line_x[g].at[high], line_sem.at[g, 1], across)
            sender.wait(from_x[g], half_sem.at[g, 0])
            add(g, 1 - y, x, 0, half, [(from_x[g], 0)])
            sender.start(mine[g].at[low, 1 - y, x], line_y[g].at[low], line_sem.at[g, 2], along)
        elif t == 2:
            sender.wait(line_x[g].at[low], line_sem.at[g, 0])
            sender.wait(line_x[g].at[high], line_sem.at[g, 1])
            sender.wait(line_y[g].at[low], line_sem.at[g, 2])
            sender.wait(line_y[g].at[high], line_sem.at[g, 3])
            add(g, y, x, 0, planes, [(line_x[g], 0), (line_y[g], 0)])
            chain(g, planes - 1)
        elif t < 1 + planes:
            chain(g, planes + 1 - t)
        else:
            land(g)

    def chain(g, k):
        for way, (at, inside, fed, target) in enumerate(
            ((z + k, z + k < planes, z > 0, up), (z - k, z - k >= 0, z < planes - 1, down))
        ):
            spot = jnp.clip(at, 0, planes - 1)

            @pl.when(both(inside, fed))
            def _(way=way, spot=spot):
                sender.wait(lines[way][g].at[spot], chain_sem.at[g, way, spot])

                def body(at, carry):
                    total = mine[g][spot, y, x, at].astype(jnp.float32)
                    total = total + lines[way][g][spot, at].astype(jnp.float32)
                    mine[g][spot, y, x, at] = total.astype(jnp.bfloat16)
                    return carry

                lax.fori_loop(0, mine[g].shape[3], body, 0)

            sender.start(
                mine[g].at[spot, y, x], lines[way][g].at[spot], chain_sem.at[g, way, spot], target, inside
            )

    def land(g):
        sender.wait(lines[0][g].at[z], chain_sem.at[g, 0, z], can_down)
        sender.wait(lines[1][g].at[z], chain_sem.at[g, 1, z], can_up)
        zero = jnp.zeros(mine[g].shape[4:], jnp.float32)

        def body(at, carry):
            total = mine[g][z, y, x, at].astype(jnp.float32)
            total = total + jnp.where(can_down, lines[0][g][z, at].astype(jnp.float32), zero)
            total = total + jnp.where(can_up, lines[1][g][z, at].astype(jnp.float32), zero)
            own[g][at] = total
            return carry

        lax.fori_loop(0, mine[g].shape[3], body, 0)

    last_scatter = planes + 1

    held, got, small_sem = r.held, r.got, r.small_sem

    def small_pairs():
        for at, peer in enumerate((partner, across, along)):
            sender.start(held.at[at], got.at[at], small_sem.at[at], peer)
            sender.wait(got.at[at], small_sem.at[at])
            held[at + 1] = held[at] + got[at]
        for peer in others:
            sender.start(held.at[3], got.at[3 + z], small_sem.at[3 + z], peer)

    def small_land():
        for k in range(1, planes):
            at = lax.rem(z + k, planes)
            sender.wait(got.at[3 + at], small_sem.at[3 + at])
        got[3 + z] = held[3]
        total = got[3]
        for zs in range(1, planes):
            total = total + got[3 + zs]
        r.small_out[...] = total

    length_row, bucket_row, table = r.length, r.bucket, r.table
    rows_in, enc, cot = r.rows, r.enc, r.cot
    positions, width = rows_in.shape
    pairs = width // LANES
    hidden = r.hid.shape[1]
    gain = r.gain

    def onehot():
        ids = lax.broadcasted_iota(jnp.int32, (table.shape[0], positions), 0)
        return (ids == bucket_row[...]).astype(jnp.float32)

    def head_lanes(which):
        lane = lax.broadcasted_iota(jnp.int32, (1, LANES), 1) // HEAD
        return (lane == which).astype(jnp.bfloat16)

    def matmul(dst, source, g):
        def body(i, col):
            weight = whole[g][:, :, :, col].reshape(-1, TILE)
            dst[:, col] = dot(source[...], weight).astype(dst.dtype)

        chunks(whole[g].shape[-1], body)

    def matmul_back(source, g):
        acc = r.acc
        count = source.shape[0]
        acc[pl.ds(0, count), :] = jnp.zeros((count, width), jnp.float32)

        def body(i, col):
            weight = whole[g][:, :, :, col].reshape(-1, TILE)
            acc[pl.ds(0, count), :] += dot(source[:, col], weight, NT)

        chunks(whole[g].shape[-1], body)
        return acc[pl.ds(0, count), :]

    def norm_forward(value, which, dst, g):
        normed, unused = rms_parts(value)
        scaled = normed * gain[pl.ds(which, 1), :]
        dst[...] = scaled.astype(jnp.bfloat16)
        turn(g, scaled)
        send_rows(g)

    def norm_back(grad, value, which):
        normed, recip = rms_parts(value)
        scaled = grad * gain[pl.ds(which, 1), :]
        held[0, pl.ds(which, 1), :] = jnp.sum(grad * normed, axis=0, keepdims=True)
        return recip * (scaled - normed * jnp.mean(scaled * normed, axis=-1, keepdims=True))

    def per_pair(body):
        def run(j, carry):
            body(j, lambda base: pl.ds(pl.multiple_of(base + j * LANES, LANES), LANES))
            return carry

        lax.fori_loop(0, pairs, run, 0)

    def start_compute():
        gain[...] = jnp.sum(whole[GAIN][...].astype(jnp.float32), axis=(0, 1))
        spread = lax.dot_general(
            table[...], onehot(), TN, precision=lax.Precision.HIGHEST, preferred_element_type=jnp.float32
        )
        r.by_dist[pl.ds(0, spread.shape[0]), :] = spread
        norm_forward(rows_in[...].astype(jnp.float32), 0, r.h1, QKV)

    def early():
        turn(KVC, enc[...].astype(jnp.float32))
        send_rows(KVC)
        send_step(FFOUT)

    def self_attention():
        matmul(r.qkv, r.h1, QKV)
        row_ids = lax.broadcasted_iota(jnp.int32, (positions, positions), 0)
        col_ids = lax.broadcasted_iota(jnp.int32, (positions, positions), 1)
        qkv = r.qkv

        def body(j, at):
            live = (col_ids <= row_ids) & (col_ids < length_row[...])
            query, key, value = qkv[:, at(0)], qkv[:, at(width)], qkv[:, at(2 * width)]
            out = jnp.zeros((positions, LANES), jnp.float32)
            for e in range(2):
                lanes = head_lanes(e)
                head = 2 * j + e
                bias = jnp.broadcast_to(r.by_dist[pl.ds(head, 1), :], (positions, positions))
                bias = pltpu.roll(bias, 0, 1, stride=1, stride_axis=0)
                scores = jnp.where(live, dot(query * lanes, key, NT) + bias, -1e30)
                top = jnp.max(scores, axis=-1, keepdims=True)
                lse = top + jnp.log(jnp.sum(jnp.exp(scores - top), axis=-1, keepdims=True))
                prob = jnp.exp(scores - lse)
                r.prob[head] = prob
                out = out + dot(prob.astype(jnp.bfloat16), value * lanes)
            r.att[:, at(0)] = out.astype(jnp.bfloat16)

        per_pair(body)
        turn(OUT, r.att[...].astype(jnp.float32))
        send_rows(OUT)

    def after_self():
        def body(i, col):
            weight = whole[OUT][:, :, :, col].reshape(-1, TILE)
            r.x1[:, col] = rows_in[:, col].astype(jnp.float32) + dot(r.att[...], weight)

        chunks(width, body)
        norm_forward(r.x1[...], 1, r.h2, QC)

    def cross_attention():
        matmul(r.kvc, enc, KVC)
        kvc = r.kvc

        def body(j, at):
            query, key, value = r.qc[:, at(0)], kvc[:, at(0)], kvc[:, at(width)]
            out = jnp.zeros((positions, LANES), jnp.float32)
            for e in range(2):
                lanes = head_lanes(e)
                scores = dot(query * lanes, key, NT)
                lse = jnp.log(jnp.sum(jnp.exp(scores), axis=-1, keepdims=True))
                prob = jnp.exp(scores - lse)
                r.prob_c[2 * j + e] = prob
                out = out + dot(prob.astype(jnp.bfloat16), value * lanes)
            r.att_c[:, at(0)] = out.astype(jnp.bfloat16)

        per_pair(body)
        turn(OUTC, r.att_c[...].astype(jnp.float32))
        send_rows(OUTC)

    def after_cross():
        def body(i, col):
            weight = whole[OUTC][:, :, :, col].reshape(-1, TILE)
            r.x2[:, col] = r.x1[:, col] + dot(r.att_c[...], weight)

        chunks(width, body)
        norm_forward(r.x2[...], 2, r.h3, FFIN)

    def feed():
        gate_up = r.gate_up
        matmul(gate_up, r.h3, FFIN)
        turned = rows_t[FFOUT]
        tall = turned.shape[2] * turned.shape[3]
        chips = TILE // (2 * tall)

        def body(i, col):
            up_col = pl.ds(pl.multiple_of(hidden + i * TILE, TILE), TILE)
            value, unused = gelu_and_slope(gate_up[:, col])
            product = value * gate_up[:, up_col]
            r.hid[:, col] = product.astype(jnp.bfloat16)
            flipped = jnp.transpose(product, (1, 0)).reshape((chips, 2) + turned.shape[2:])
            flipped = flipped.astype(jnp.bfloat16)
            turned[0, pl.ds(i * chips, chips)] = flipped[:, 0]
            turned[1, pl.ds(i * chips, chips)] = flipped[:, 1]

        chunks(hidden, body)
        send_rows(FFOUT)

    def feed_back():
        gate_up, change = r.gate_up, step[FFIN]
        tall = whole[FFOUT].shape[1] * SUB
        devices = TILE // tall

        def body(i, col):
            up_col = pl.ds(pl.multiple_of(hidden + i * TILE, TILE), TILE)
            weight = whole[FFOUT][pl.ds(i * devices, devices)].reshape(TILE, width)
            d_hidden = dot(cot[...], weight, NT)
            value, slope = gelu_and_slope(gate_up[:, col])
            change[:, col] = (d_hidden * gate_up[:, up_col] * slope).astype(jnp.bfloat16)
            change[:, up_col] = (d_hidden * value).astype(jnp.bfloat16)

        chunks(hidden, body)
        send_step(FFIN)

    def finish_forward():
        def body(i, col):
            weight = whole[FFOUT][:, :, :, col].reshape(-1, TILE)
            r.result[:, col] = (r.x2[:, col] + dot(r.hid[...], weight)).astype(jnp.bfloat16)

        chunks(width, body)

    def before_cross():
        back = norm_back(matmul_back(step[FFIN], FFIN), r.x2[...], 2)
        r.dx[...] = cot[...].astype(jnp.float32) + back
        step[OUTC][...] = r.dx[...].astype(jnp.bfloat16)
        send_step(OUTC)

    def cross_attention_back():
        d_att = matmul_back_rows(step[OUTC], OUTC)
        kvc = r.kvc

        def body(j, at):
            query, key, value = r.qc[:, at(0)], kvc[:, at(0)], kvc[:, at(width)]
            grad, out = d_att[:, at(0)], r.att_c[:, at(0)].astype(jnp.float32)
            grads = attend_pair_back(j, query, key, value, grad, out, r.prob_c, None)
            step[QC][:, at(0)] = grads[0].astype(jnp.bfloat16)
            step[KVC][:, at(0)] = grads[1].astype(jnp.bfloat16)
            step[KVC][:, at(width)] = grads[2].astype(jnp.bfloat16)

        per_pair(body)
        send_step(KVC)
        send_step(QC)

    def matmul_back_rows(source, g):
        r.d_att[...] = matmul_back(source, g)
        return r.d_att

    def attend_pair_back(j, query, key, value, grad, out, probs, spread):
        grad_b = grad.astype(jnp.bfloat16)
        d_query, d_key, d_value = 0.0, 0.0, 0.0
        for e in range(2):
            lanes = head_lanes(e)
            prob = probs[2 * j + e]
            inside = lax.broadcasted_iota(jnp.int32, (positions, LANES), 1) // HEAD == e
            delta = jnp.sum(jnp.where(inside, grad * out, 0.0), axis=-1, keepdims=True)
            d_prob = dot(grad_b * lanes, value, NT)
            d_score = prob * (d_prob - delta)
            if spread is not None:
                spread(2 * j + e, d_score)
            d_score_b = d_score.astype(jnp.bfloat16)
            d_value = d_value + dot(prob.astype(jnp.bfloat16), grad_b * lanes, TN)
            d_query = d_query + dot(d_score_b, key * lanes)
            d_key = d_key + dot(d_score_b, query * lanes, TN)
        return d_query, d_key, d_value

    def between():
        r.enc_grad[...] = matmul_back(step[KVC], KVC).astype(jnp.bfloat16)
        back = norm_back(matmul_back(step[QC], QC), r.x1[...], 1)
        r.dx[...] += back
        step[OUT][...] = r.dx[...].astype(jnp.bfloat16)
        send_step(OUT)

    def self_attention_back():
        d_att = matmul_back_rows(step[OUT], OUT)
        qkv = r.qkv
        row = lax.broadcasted_iota(jnp.int32, (SUB, positions), 0)

        def spread(head, d_score):
            total, count = d_score, positions // 2
            while count >= SUB:
                total = total[:count] + pltpu.roll(total[count:], positions - count, 1)
                count //= 2
            for bit in (4, 2, 1):
                total = jnp.where(
                    lax.rem(row // bit, 2) == 1, pltpu.roll(total, positions - bit, 1), total
                )
            r.by_dist[pl.ds(head, 1), :] = jnp.sum(total, axis=0, keepdims=True)

        def body(j, at):
            query, key, value = qkv[:, at(0)], qkv[:, at(width)], qkv[:, at(2 * width)]
            grad, out = d_att[:, at(0)], r.att[:, at(0)].astype(jnp.float32)
            grads = attend_pair_back(j, query, key, value, grad, out, r.prob, spread)
            for part in range(3):
                step[QKV][:, at(part * width)] = grads[part].astype(jnp.bfloat16)

        per_pair(body)
        send_step(QKV)

    def last():
        back = norm_back(matmul_back(step[QKV], QKV), rows_in[...].astype(jnp.float32), 0)
        r.input_grad[...] = (r.dx[...] + back).astype(jnp.bfloat16)
        sums = lax.dot_general(
            r.by_dist[...], onehot(), NT, precision=lax.Precision.HIGHEST,
            preferred_element_type=jnp.float32,
        )
        held[0, pl.ds(SUB, sums.shape[0]), pl.ds(0, sums.shape[1])] = sums

    held[0] = jnp.zeros(held.shape[1:], jnp.float32)
    r.by_dist[...] = jnp.zeros(r.by_dist.shape, jnp.float32)
    gathers = {GAIN: 0, QKV: 0, OUT: 2, QC: 2, KVC: 3, OUTC: 4, FFIN: 5, FFOUT: 7}
    ready = {
        GAIN: start_compute,
        QKV: self_attention,
        OUT: after_self,
        QC: lambda: matmul(r.qc, r.h2, QC),
        KVC: cross_attention,
        OUTC: after_cross,
        FFIN: feed,
    }
    for now in range(max(gathers.values()) + planes + 2):
        for g, begin in gathers.items():
            if 0 <= now - begin < planes + 2:
                gather_stage(g, now - begin)
        if now == 0:
            early()
        for g, begin in gathers.items():
            if now - begin == planes + 1 and g != FFOUT:
                settle(g)
                ready[g]()
    weight_grad(FFOUT)
    settle(FFOUT)
    slots = [
        (feed_back, FFOUT),
        (before_cross, None),
        (lambda: weight_grad(FFIN), FFIN),
        (finish_forward, None),
        (cross_attention_back, None),
        (lambda: weight_grad(OUTC), OUTC),
        (between, None),
        (lambda: (weight_grad(KVC), weight_grad(QC)), (KVC, QC)),
        (self_attention_back, None),
        (lambda: weight_grad(OUT), OUT),
        (last, None),
        (lambda: weight_grad(QKV), QKV),
        (small_pairs, None),
    ]
    begun = {FFOUT: 0}
    scatter_stage(FFOUT, 0)
    now = 0
    while now < len(slots) or any(now - b <= last_scatter for b in begun.values()):
        if now < len(slots):
            work, groups = slots[now]
            work()
            if groups is not None and groups != FFOUT:
                for g in groups if isinstance(groups, tuple) else (groups,):
                    begun[g] = now
                    scatter_stage(g, 0)
        for g, begin in begun.items():
            if 1 <= now - begin <= last_scatter:
                scatter_stage(g, now - begin)
        now += 1
    small_land()
    sender.finish()


def per_device(
    inputs, encoded, lengths, bucket_ids, qkv_weights, out_weights, ff_in, ff_out, gains, bias_table, cotangent
):
    count = lax.axis_size("fsdp")
    me = lax.axis_index("fsdp")
    planes = count // 8
    half = planes // 2
    depth, width, hidden = qkv_weights.shape[0], qkv_weights.shape[-1], ff_in.shape[-1]
    positions, keys = inputs.shape[1], encoded.shape[1]
    heads, buckets = bias_table.shape[1], bias_table.shape[0]
    gain_row = lax.dynamic_update_slice(
        jnp.zeros((SUB, width), jnp.bfloat16), gains, (jnp.int32(0), me * gains.shape[1])
    )
    shards = [
        gain_row,
        qkv_weights[:, 0:3].reshape(depth, 3 * width),
        out_weights[:, 0],
        qkv_weights[:, 3],
        qkv_weights[:, 4:6].reshape(depth, 2 * width),
        out_weights[:, 1],
        ff_in.reshape(depth, 2 * hidden),
        ff_out,
    ]
    shards = [s.reshape(-1, SUB, s.shape[-1]) for s in shards]
    backward_ids = jnp.concatenate([bucket_ids[:1], bucket_ids[:0:-1]])[None]
    length_row = jnp.broadcast_to(lengths[:, None], (1, positions))
    bf, fl = jnp.bfloat16, jnp.float32
    any_spec, vmem = pl.BlockSpec(memory_space=pl.ANY), pl.BlockSpec(memory_space=pltpu.VMEM)
    ins = dict(
        shard=shards,
        rows=inputs[0],
        enc=encoded[0],
        cot=cotangent[0],
        length=length_row,
        bucket=backward_ids,
        table=bias_table,
    )
    in_specs = [any_spec if s.ndim == 3 else vmem for s in jax.tree.leaves(ins)]
    padded = 2 * SUB * -(-heads // (2 * SUB))
    small = (SUB + padded, width)
    square = (positions, width)
    kinds = range(1, 8)
    shape = jax.ShapeDtypeStruct
    outs = dict(
        result=shape(square, bf),
        input_grad=shape(square, bf),
        enc_grad=shape((keys, width), bf),
        small_out=shape(small, fl),
        own=[shape(shards[g].shape, fl) for g in kinds],
    )
    room, sems = pltpu.VMEM, pltpu.SemaphoreType.DMA
    tokens = [keys if g == KVC else positions for g in range(8)]
    blocks = [s.shape for s in shards]
    chips = count // 2

    def rows_room(lead, g):
        return room(lead + (chips, blocks[g][0], SUB, tokens[g]), bf)

    def block_rooms(*lead):
        return [room(lead + blocks[g], bf) for g in kinds]

    rooms = dict(
        whole=[room((count,) + b, bf) for b in blocks],
        turned=[rows_room((2,), g) for g in kinds],
        turned_p=[rows_room((), g) for g in kinds],
        step=[room((tokens[g], blocks[g][2]), bf) for g in kinds if g != FFOUT],
        step_p=[room((tokens[g], blocks[g][2]), bf) for g in kinds],
        mine=block_rooms(planes, 2, 2),
        from_x=block_rooms(half),
        from_y=block_rooms(planes - half),
        line_x=block_rooms(planes),
        line_y=block_rooms(planes),
        line_u=block_rooms(planes),
        line_d=block_rooms(planes),
        gain=room((SUB, width), fl),
        by_dist=room((padded, positions), fl),
        h1=room(square, bf),
        h2=room(square, bf),
        h3=room(square, bf),
        qkv=room((positions, 3 * width), bf),
        qc=room(square, bf),
        kvc=room((keys, 2 * width), bf),
        att=room(square, bf),
        att_c=room(square, bf),
        prob=room((heads, positions, positions), fl),
        prob_c=room((heads, positions, keys), fl),
        x1=room(square, fl),
        x2=room(square, fl),
        dx=room(square, fl),
        acc=room(square, fl),
        d_att=room(square, fl),
        gate_up=room((positions, 2 * hidden), fl),
        hid=room((positions, hidden), bf),
        held=room((4,) + small, fl),
        got=room((3 + planes,) + small, fl),
        local_sem=sems((8,)),
        send_sem=sems((8 * (10 * planes + 8 * planes - 8) + 7 * (4 + 2 * planes) + 16 + planes,)),
        recv_sem=sems((8, count)),
        pair_sem=sems((8, 2)),
        half_sem=sems((8, 2)),
        line_sem=sems((8, 4)),
        chain_sem=sems((8, 2, planes)),
        small_sem=sems((3 + planes,)),
    )

    in_leaves, out_leaves, room_leaves = jax.tree.leaves(ins), jax.tree.leaves(outs), jax.tree.leaves(rooms)
    sizes = [len(in_leaves), len(out_leaves), len(room_leaves)]
    at = iter(range(sum(sizes)))
    order = {}
    for part in (ins, outs, rooms):
        order.update(jax.tree.map(lambda unused: next(at), part))
    numbers, tree = jax.tree.flatten(order)
    done = pl.pallas_call(
        lambda *refs: layer_kernel(planes, tree, *[refs[i] for i in numbers]),
        out_shape=out_leaves,
        in_specs=in_specs,
        out_specs=[vmem] * len(out_leaves),
        scratch_shapes=room_leaves,
        compiler_params=pltpu.CompilerParams(
            collective_id=0, has_side_effects=True, vmem_limit_bytes=62 * 1024 * 1024
        ),
        name="layer",
    )(*in_leaves)
    done = types.SimpleNamespace(**jax.tree.unflatten(jax.tree.structure(outs), done))
    result, dx, enc_grad, total = done.result, done.input_grad, done.enc_grad, done.small_out
    done = done.own
    o_qkv, o_o, o_qc, o_kvc, o_oc, o_in, o_out = (o.reshape(-1, o.shape[-1]) for o in done)
    s_gain = lax.dynamic_slice(
        total[: gains.shape[0]], (jnp.int32(0), me * gains.shape[1]), gains.shape
    )
    s_table = jnp.transpose(total[SUB : SUB + heads, :buckets])
    return (
        result[None],
        dx[None],
        enc_grad[None],
        jnp.concatenate([o_qkv, o_qc, o_kvc], axis=1).reshape(qkv_weights.shape),
        jnp.concatenate([o_o, o_oc], axis=1).reshape(out_weights.shape),
        o_in.reshape(ff_in.shape),
        o_out,
        s_gain,
        s_table,
    )


def solution(mesh):
    count = mesh.shape["fsdp"]

    def layer(*args):
        depth, tall = args[4].shape[0], args[7].shape[0]
        tiled = depth % SUB == 0 and tall % SUB == 0 and count % 8 == 0 and count > 8
        tiled = tiled and TILE % (2 * tall) == 0 and args[0].shape[1] == LANES and LANES == 2 * HEAD
        return (per_device if tiled else plain_device)(*args)

    rows, split = P("fsdp", None, None), P("fsdp", None)
    return jax.shard_map(
        layer,
        mesh=mesh,
        in_specs=(rows, rows, P("fsdp"), P(), rows, rows, rows, split, P(None, "fsdp"), P(), rows),
        out_specs=(rows, rows, rows, rows, rows, rows, split, P(None, "fsdp"), P()),
        check_vma=False,
    )
```

```python
import types

import jax
import jax.numpy as jnp
from jax import lax
from jax.experimental import pallas as pl
from jax.experimental.pallas import tpu as pltpu
from jax.sharding import PartitionSpec as P

HEAD = 64


EPS = 1e-06


def prod(form, left, right):
    return jnp.einsum(form, left, right, preferred_element_type=jnp.float32)


def gelu_tanh(value):
    return (
        0.5
        * value
        * (1.0 + jnp.tanh(0.7978845608028654 * (value + 0.044715 * value * value * value)))
    )


def rms_fwd(value, gain):
    recip = lax.rsqrt(jnp.mean(value * value, axis=-1, keepdims=True) + EPS)
    normed = value * recip
    return ((normed * gain).astype(jnp.bfloat16), normed, recip)


def rms_bwd(grad, normed, recip, gain):
    scaled = grad * gain
    gain_grad = jnp.sum(grad * normed, axis=0)
    back = recip * (scaled - normed * jnp.mean(scaled * normed, axis=-1, keepdims=True))
    return (back, gain_grad)


def toeplitz_bias(bucket_ids, table, positions):
    onehot = (bucket_ids[:, None] == jnp.arange(table.shape[0], dtype=jnp.int32)[None, :]).astype(
        jnp.float32
    )
    by_dist = jnp.transpose(jnp.dot(onehot, table, precision=lax.Precision.HIGHEST), (1, 0))
    head_count = by_dist.shape[0]
    nearest = jnp.broadcast_to(by_dist[:, 0:1], (head_count, positions))
    cyclic = jnp.concatenate(
        [nearest, jnp.zeros((head_count, 1), jnp.float32), by_dist[:, :0:-1]], axis=1
    )
    tiled = jnp.broadcast_to(cyclic[:, None, :], (head_count, positions, 2 * positions))
    tiled = tiled.reshape(head_count, 2 * positions * positions)
    skewed = tiled[:, : positions * (2 * positions - 1)].reshape(
        head_count, positions, 2 * positions - 1
    )
    return (skewed[:, :, :positions], onehot)


def diagonal_sums(d_score, onehot):
    head_count, positions = (d_score.shape[0], d_score.shape[1])
    padded = jnp.pad(d_score, ((0, 0), (0, 0), (0, positions - 1)))
    padded = padded.reshape(head_count, positions * (2 * positions - 1))
    padded = jnp.pad(padded, ((0, 0), (0, positions))).reshape(head_count, positions, 2 * positions)
    column = jnp.sum(padded, axis=1)
    by_dist = jnp.concatenate(
        [jnp.sum(column[:, :positions], axis=1, keepdims=True), column[:, :positions:-1]], axis=1
    )
    return jnp.dot(
        jnp.transpose(onehot, (1, 0)),
        jnp.transpose(by_dist, (1, 0)),
        precision=lax.Precision.HIGHEST,
    )


def scores_of(query, keys, bias, mask):
    rows = query.shape[0]
    q3 = query.reshape(rows, -1, HEAD)
    k3 = keys.reshape(keys.shape[0], -1, HEAD)
    scores = prod("qhd,khd->hqk", q3, k3)
    if bias is not None:
        scores = scores + bias
    if mask is not None:
        scores = jnp.where(mask[None], scores, -1e30)
    return scores


def attend(query, keys, values, bias, mask, shifted):
    rows = query.shape[0]
    scores = scores_of(query, keys, bias, mask)
    if shifted:
        top = jnp.max(scores, axis=-1, keepdims=True)
        lse = top + jnp.log(jnp.sum(jnp.exp(scores - top), axis=-1, keepdims=True))
    else:
        lse = jnp.log(jnp.sum(jnp.exp(scores), axis=-1, keepdims=True))
    prob = jnp.exp(scores - lse).astype(jnp.bfloat16)
    v3 = values.reshape(values.shape[0], -1, HEAD)
    out = prod("hqk,khd->qhd", prob, v3).reshape(rows, -1).astype(jnp.bfloat16)
    return (out, lse)


def attend_back(query, keys, values, out, lse, grad_out, bias, mask):
    rows = query.shape[0]
    scores = scores_of(query, keys, bias, mask)
    prob = jnp.exp(scores - lse)
    prob_b = prob.astype(jnp.bfloat16)
    q3 = query.reshape(rows, -1, HEAD)
    k3 = keys.reshape(keys.shape[0], -1, HEAD)
    v3 = values.reshape(values.shape[0], -1, HEAD)
    grad3 = grad_out.reshape(rows, -1, HEAD)
    grad_b = grad3.astype(jnp.bfloat16)
    out3 = out.reshape(rows, -1, HEAD).astype(jnp.float32)
    d_val = prod("hqk,qhd->khd", prob_b, grad_b)
    d_prob = prod("qhd,khd->hqk", grad_b, v3)
    delta = jnp.transpose(jnp.sum(grad3 * out3, axis=2), (1, 0))
    d_score = prob * (d_prob - delta[:, :, None])
    d_score_b = d_score.astype(jnp.bfloat16)
    d_query = prod("hqk,khd->qhd", d_score_b, k3)
    d_key = prod("hqk,qhd->khd", d_score_b, q3)
    shape_q = (rows, -1)
    shape_k = (keys.shape[0], -1)
    return (
        d_query.reshape(shape_q).astype(jnp.bfloat16),
        d_key.reshape(shape_k).astype(jnp.bfloat16),
        d_val.reshape(shape_k).astype(jnp.bfloat16),
        d_score,
    )


def forward(rows, enc, length, bucket_ids, weights, table):
    qkv_w, out_w, ff_in, ff_out, gains = weights
    positions = rows.shape[0]
    gain_f = gains.astype(jnp.float32)
    start = rows.astype(jnp.float32)
    h1, n1, r1 = rms_fwd(start, gain_f[0])
    qkv = prod("ld,cde->cle", h1, qkv_w[0:3]).astype(jnp.bfloat16)
    row_ids = lax.broadcasted_iota(jnp.int32, (positions, positions), 0)
    col_ids = lax.broadcasted_iota(jnp.int32, (positions, positions), 1)
    mask = (col_ids <= row_ids) & (col_ids < length)
    bias, onehot = toeplitz_bias(bucket_ids, table, positions)
    a1, lse1 = attend(qkv[0], qkv[1], qkv[2], bias, mask, True)
    x1 = start + prod("le,ed->ld", a1, out_w[0])
    h2, n2, r2 = rms_fwd(x1, gain_f[1])
    qc = prod("ld,de->le", h2, qkv_w[3]).astype(jnp.bfloat16)
    kvc = prod("ld,cde->cle", enc, qkv_w[4:6]).astype(jnp.bfloat16)
    ac, lse2 = attend(qc, kvc[0], kvc[1], None, None, False)
    x2 = x1 + prod("le,ed->ld", ac, out_w[1])
    h3, n3, r3 = rms_fwd(x2, gain_f[2])
    gate_up = prod("ld,cdf->clf", h3, ff_in)
    hidden = (gelu_tanh(gate_up[0]) * gate_up[1]).astype(jnp.bfloat16)
    result = x2 + prod("lf,fd->ld", hidden, ff_out)
    saved = (
        h1,
        n1,
        r1,
        qkv,
        bias,
        mask,
        a1,
        lse1,
        h2,
        n2,
        r2,
        qc,
        kvc,
        ac,
        lse2,
        h3,
        n3,
        r3,
        gate_up,
        hidden,
        onehot,
    )
    return (result.astype(jnp.bfloat16), saved)


def ff_back(saved, weights, cot):
    qkv_w, out_w, ff_in, ff_out, gains = weights
    gain_f = gains.astype(jnp.float32)
    h3, n3, r3, gate_up, hidden = (saved[15], saved[16], saved[17], saved[18], saved[19])
    d_ffout = prod("lf,ld->fd", hidden, cot)
    d_hidden = prod("ld,fd->lf", cot, ff_out)
    gelu_val, gelu_pull = jax.vjp(gelu_tanh, gate_up[0])
    d_gate = gelu_pull(d_hidden * gate_up[1])[0]
    d_up = d_hidden * gelu_val
    d_gate_up = jnp.stack([d_gate, d_up]).astype(jnp.bfloat16)
    d_ffin = prod("ld,clf->cdf", h3, d_gate_up)
    d_h3 = prod("clf,cdf->ld", d_gate_up, ff_in)
    back3, gain3 = rms_bwd(d_h3, n3, r3, gain_f[2])
    return (cot.astype(jnp.float32) + back3, d_ffin, d_ffout, gain3)


def cross_back(saved, weights, enc, dx2):
    qkv_w, out_w, ff_in, ff_out, gains = weights
    gain_f = gains.astype(jnp.float32)
    h2, n2, r2, qc, kvc, ac, lse2 = (
        saved[8],
        saved[9],
        saved[10],
        saved[11],
        saved[12],
        saved[13],
        saved[14],
    )
    dx2_b = dx2.astype(jnp.bfloat16)
    d_outc = prod("le,ld->ed", ac, dx2_b)
    d_ac = prod("ld,ed->le", dx2_b, out_w[1])
    d_qc, d_kc, d_vc, unused = attend_back(qc, kvc[0], kvc[1], ac, lse2, d_ac, None, None)
    g_qc = prod("ld,le->de", h2, d_qc)
    d_kvc = jnp.stack([d_kc, d_vc])
    g_kvc = prod("ld,cle->cde", enc, d_kvc)
    enc_grad = prod("cle,cde->ld", d_kvc, qkv_w[4:6]).astype(jnp.bfloat16)
    d_h2 = prod("le,de->ld", d_qc, qkv_w[3])
    back2, gain2 = rms_bwd(d_h2, n2, r2, gain_f[1])
    return (dx2 + back2, g_qc, g_kvc, d_outc, gain2, enc_grad)


def self_back(saved, weights, dx1):
    qkv_w, out_w, ff_in, ff_out, gains = weights
    gain_f = gains.astype(jnp.float32)
    h1, n1, r1, qkv, bias, mask, a1, lse1 = saved[0:8]
    onehot = saved[20]
    dx1_b = dx1.astype(jnp.bfloat16)
    d_outs = prod("le,ld->ed", a1, dx1_b)
    d_a1 = prod("ld,ed->le", dx1_b, out_w[0])
    d_q, d_k, d_v, d_score = attend_back(qkv[0], qkv[1], qkv[2], a1, lse1, d_a1, bias, mask)
    d_qkv = jnp.stack([d_q, d_k, d_v])
    g_qkv = prod("ld,cle->cde", h1, d_qkv)
    d_h1 = prod("cle,cde->ld", d_qkv, qkv_w[0:3])
    back1, gain1 = rms_bwd(d_h1, n1, r1, gain_f[0])
    d_table = diagonal_sums(d_score, onehot)
    return ((dx1 + back1).astype(jnp.bfloat16), g_qkv, d_outs, gain1, d_table)


def to_blocks(array, width):
    blocks = []
    for copy in range(array.shape[0]):
        for start in range(0, array.shape[-1], width):
            block = array[copy, ..., start : start + width]
            short = width - block.shape[-1]
            if short:
                block = jnp.pad(block, ((0, 0),) * (block.ndim - 1) + ((0, short),))
            blocks.append(block)
    return blocks


def from_blocks(blocks, shape, width):
    copies, rows, columns = shape
    each = -(-columns // width)
    planes = []
    for copy in range(copies):
        part = [blocks[copy * each + at] for at in range(each)]
        part[-1] = part[-1][..., : columns - (each - 1) * width]
        planes.append(part[0] if each == 1 else jnp.concatenate(part, axis=-1))
    return planes


def plain_device(
    inputs,
    encoded,
    lengths,
    bucket_ids,
    qkv_weights,
    out_weights,
    ff_in,
    ff_out,
    gains,
    bias_table,
    cotangent,
):
    count = lax.axis_size("fsdp")
    shards = (
        jnp.transpose(qkv_weights, (1, 0, 2)),
        jnp.transpose(out_weights, (1, 0, 2)),
        jnp.transpose(ff_in, (1, 0, 2)),
        ff_out[None],
    )
    width = qkv_weights.shape[-1]
    depth = qkv_weights.shape[0]
    tall = ff_out.shape[0]
    blocks = to_blocks(shards[0], width) + to_blocks(shards[1], width) + to_blocks(shards[2], width)
    slots = gains.size
    tail = 8 * -(-slots // (8 * width))
    gain_rows = jnp.pad(gains.reshape(1, slots), ((0, 0), (0, tail * width - slots)))
    packed = jnp.concatenate(blocks + [ff_out, gain_rows.reshape(tail, width)], axis=0)
    whole = lax.all_gather(packed, "fsdp", axis=0, tiled=False)
    cut = len(blocks) * depth
    stacked = whole[:, :cut].reshape(count, len(blocks), depth, width)
    stacked = jnp.transpose(stacked, (1, 0, 2, 3)).reshape(len(blocks), count * depth, width)
    ff_out_all = whole[:, cut : cut + tall].reshape(count * tall, width)
    stacked, ff_out_all = lax.optimization_barrier((stacked, ff_out_all))
    n_qkv, n_out = qkv_weights.shape[1], out_weights.shape[1]
    ff_all = jnp.stack(from_blocks(stacked[n_qkv + n_out :], shards[2].shape, width))
    main = (stacked[:n_qkv], stacked[n_qkv : n_qkv + n_out], ff_all, ff_out_all[None])
    gain_all = whole[:, -tail:].reshape(count, tail * width)[:, :slots]
    gain_all = gain_all.reshape(count, gains.shape[0], gains.shape[1])
    gain_all = jnp.transpose(gain_all, (1, 0, 2)).reshape(gains.shape[0], -1)
    weights = (main[0], main[1], main[2], main[3][0], gain_all)
    result, saved = forward(inputs[0], encoded[0], lengths[0], bucket_ids, weights, bias_table)
    dx2, g_ffin, g_ffout, gain3 = ff_back(saved, weights, cotangent[0])
    dx1, g_qc, g_kvc, g_outc, gain2, enc_grad = cross_back(saved, weights, encoded[0], dx2)
    dx, g_qkvs, g_outs, gain1, g_table = self_back(saved, weights, dx1)
    wide = [g_qkvs[0], g_qkvs[1], g_qkvs[2], g_qc, g_kvc[0], g_kvc[1], g_outs, g_outc]
    wide += to_blocks(g_ffin, width)
    wide.append(g_ffout)
    g_gain = jnp.stack([gain1, gain2, gain3]).reshape(gains.shape[0], count, -1)
    g_gain = jnp.transpose(g_gain, (1, 0, 2)).reshape(count, slots)
    g_gain = jnp.pad(g_gain, ((0, 0), (0, tail * width - slots))).reshape(count, tail, width)
    parts = [grad.astype(jnp.bfloat16).reshape(count, -1, width) for grad in wide]
    send = jnp.concatenate(parts + [g_gain.astype(jnp.bfloat16)], axis=1)
    send, g_table = lax.optimization_barrier((send, g_table))
    own = lax.psum_scatter(send, "fsdp", scatter_dimension=0, tiled=False).astype(jnp.float32)
    mine = own[:cut].reshape(len(blocks), depth, width)
    s_ffin = jnp.stack(from_blocks(mine[n_qkv + n_out :], shards[2].shape, width))
    s_main = (mine[:n_qkv], mine[n_qkv : n_qkv + n_out], s_ffin, own[cut : cut + tall][None])
    s_gain = own[-tail:].reshape(tail * width)[:slots].reshape(gains.shape)
    s_table = lax.psum(g_table, "fsdp")
    return (
        result[None],
        dx[None],
        enc_grad[None],
        jnp.transpose(s_main[0], (1, 0, 2)),
        jnp.transpose(s_main[1], (1, 0, 2)),
        jnp.transpose(s_main[2], (1, 0, 2)),
        s_main[3][0],
        s_gain,
        s_table,
    )


MESH = pl.DeviceIdType.MESH
SUB, LANES, TILE = 8, 128, 256
GAIN, QKV, OUT, QC, KVC, OUTC, FFIN, FFOUT = range(8)
NT = (((1,), (1,)), ((), ()))
TN = (((0,), (0,)), ((), ()))
NN = (((1,), (0,)), ((), ()))


def dot(left, right, dims=NN):
    return lax.dot_general(left, right, dims, preferred_element_type=jnp.float32)


def place():
    me = lax.axis_index("fsdp")
    return me, lax.rem(me, 2), lax.rem(me // 2, 2), lax.rem(me // 4, 2), me // 8


def device(z, y, x, core):
    return ((z * 2 + y) * 2 + x) * 2 + core


def both(first, second):
    if first is None:
        return second
    if second is None:
        return first
    return jnp.logical_and(first, second)


def maybe(cond, action):
    if cond is None:
        action()
    else:
        pl.when(cond)(action)


class Sender:
    def __init__(self, sems, anyone):
        self.sems = sems
        self.anyone = anyone
        self.used = 0
        self.open = []

    def start(self, src, dst, recv, target, cond=None):
        copy = pltpu.make_async_remote_copy(
            src_ref=src,
            dst_ref=dst,
            send_sem=self.sems.at[self.used],
            recv_sem=recv,
            device_id=(target,),
            device_id_type=MESH,
        )
        self.used += 1
        self.open.append((cond, copy))
        maybe(cond, copy.start)

    def wait(self, dst, sem, cond=None):
        copy = pltpu.make_async_remote_copy(
            src_ref=dst,
            dst_ref=dst,
            send_sem=self.sems.at[0],
            recv_sem=sem,
            device_id=(self.anyone,),
            device_id_type=MESH,
        )
        maybe(cond, copy.wait_recv)

    def finish(self):
        for cond, copy in self.open:
            maybe(cond, copy.wait_send)


def chunks(total, body):
    def step(i, carry):
        body(i, pl.ds(pl.multiple_of(i * TILE, TILE), TILE))
        return carry

    lax.fori_loop(0, total // TILE, step, 0)


def rms_parts(value):
    recip = lax.rsqrt(jnp.mean(value * value, axis=-1, keepdims=True) + EPS)
    return value * recip, recip


def gelu_and_slope(value):
    inner = 0.7978845608028654 * (value + 0.044715 * value * value * value)
    bent = jnp.tanh(inner)
    slope = 0.5 * (1.0 + bent) + 0.5 * value * (1.0 - bent * bent) * (
        0.7978845608028654 * (1.0 + 3.0 * 0.044715 * value * value)
    )
    return 0.5 * value * (1.0 + bent), slope


def layer_kernel(planes, tree, *refs):
    r = types.SimpleNamespace(**jax.tree.unflatten(tree, refs))
    me, core, x, y, z = place()
    partner, across, along = device(z, y, x, 1 - core), device(z, y, 1 - x, core), device(z, 1 - y, x, core)
    up, down = device(z + 1, y, x, core), device(z - 1, y, x, core)
    can_up, can_down = z < planes - 1, z > 0
    half = planes // 2
    others = [device(lax.rem(z + k, planes), y, x, core) for k in range(1, planes)]
    whole = r.whole
    wide = r.rows.shape[1]
    gain_in, qkv_in, out_in, ff_in, ff_out = r.shard
    shard = [
        gain_in,
        qkv_in.at[:, :, pl.ds(0, 3 * wide)],
        out_in.at[:, :, pl.ds(0, wide)],
        qkv_in.at[:, :, pl.ds(3 * wide, wide)],
        qkv_in.at[:, :, pl.ds(4 * wide, 2 * wide)],
        out_in.at[:, :, pl.ds(wide, wide)],
        ff_in,
        ff_out,
    ]
    qkv_own, out_own, in_own, down_own = r.own
    own = [
        None,
        (qkv_own, 0),
        (out_own, 0),
        (qkv_own, 3 * wide),
        (qkv_own, 4 * wide),
        (out_own, wide),
        (in_own, 0),
        (down_own, 0),
    ]
    local_sem, recv_sem, pair_sem, share_sem = r.local_sem, r.recv_sem, r.pair_sem, r.share_sem
    sender = Sender(r.send_sem, partner)

    def load_own(g):
        return pltpu.make_async_copy(shard[g], whole[g].at[me], local_sem.at[g])

    for g in range(8):
        load_own(g).start()
    barrier = pltpu.get_barrier_semaphore()
    peers = [partner, across, along, *others]
    for peer in peers:
        pl.semaphore_signal(barrier, inc=1, device_id=(peer,), device_id_type=MESH)
    pl.semaphore_wait(barrier, len(peers))

    def send(g, src, target, cond, own=False):
        sender.start(
            shard[g] if own else whole[g].at[src], whole[g].at[src], recv_sem.at[g, src], target, cond
        )

    def arrive(g, src, cond=None):
        sender.wait(whole[g].at[src], recv_sem.at[g, src], cond)

    def steps(k):
        if k == 0:
            return [(None, z)]
        return [(z - k >= 0, z - k), (z + k < planes, z + k)]

    def line(g, k):
        for side, (cond, zs) in enumerate(steps(k)):
            src = device(zs, y, x, core)
            if k:
                arrive(g, src, cond)
            if k == 0 or side == 0:
                send(g, src, up, both(cond, can_up), k == 0)
            if k == 0 or side == 1:
                send(g, src, down, both(cond, can_down), k == 0)
            send(g, src, across, cond, k == 0)
            send(g, src, along, cond, k == 0)
            send(g, src, partner, cond, k == 0)

    def shares(g):
        deep = whole[g].shape[1]
        by_line = deep // 3
        return (0, deep - 2 * by_line), (deep - 2 * by_line, by_line), (deep - by_line, by_line)

    def send_share(g, src, which, sem, target, cond):
        first, number = shares(g)[which]
        if number:
            part = whole[g].at[src, pl.ds(first, number)]
            sender.start(part, part, sem, target, cond)

    def arrive_share(g, src, which, sem, cond):
        first, number = shares(g)[which]
        if number:
            sender.wait(whole[g].at[src, pl.ds(first, number)], sem, cond)

    def plane(g, k):
        for cond, zs in steps(k):
            src = device(zs, y, 1 - x, core)
            arrive(g, src, cond)
            send_share(g, src, 0, recv_sem.at[g, src], along, both(cond, zs >= half))
            if k == 0:
                send_share(g, src, 2, share_sem.at[g, 1, z], along, cond)
            send(g, src, partner, cond)
            src = device(zs, 1 - y, x, core)
            arrive(g, src, cond)
            send_share(g, src, 0, recv_sem.at[g, src], across, both(cond, zs < half))
            if k == 0:
                send_share(g, src, 1, share_sem.at[g, 0, z], across, cond)
            send(g, src, partner, cond)

    def corner(g, k):
        for side, (cond, zs) in enumerate(steps(k)):
            src = device(zs, 1 - y, 1 - x, core)
            spot = zs if cond is None else jnp.clip(zs, 0, planes - 1)
            for way in range(2):
                sem = share_sem.at[g, way, spot]
                arrive_share(g, src, way + 1, sem, cond)
                if k == 0 or side == 0:
                    send_share(g, src, way + 1, sem, up, both(cond, can_up))
                if k == 0 or side == 1:
                    send_share(g, src, way + 1, sem, down, both(cond, can_down))
            arrive_share(g, src, 0, recv_sem.at[g, src], cond)
            send(g, src, partner, cond)

    def gather_stage(g, t):
        if t < planes:
            line(g, t)
        if 0 <= t - 1 < planes:
            plane(g, t - 1)
        if 0 <= t - 2 < planes:
            corner(g, t - 2)

    def settle(g):
        for zs in range(planes):
            for ys in range(2):
                for xs in range(2):
                    arrive(g, device(zs, ys, xs, 1 - core))
        load_own(g).wait()

    rows_t, rows_p, step_p, mine = ([None] + list(a) for a in (r.turned, r.turned_p, r.step_p, r.mine))
    step = [None] + list(r.step) + [r.cot]

    def turn(g, value):
        shape = rows_t[g].shape
        turned = jnp.transpose(value, (1, 0)).reshape((shape[1], 2) + shape[2:]).astype(jnp.bfloat16)
        rows_t[g][0] = turned[:, 0]
        rows_t[g][1] = turned[:, 1]

    def send_rows(g):
        sender.start(rows_t[g].at[1 - core], rows_p[g], pair_sem.at[g, 0], partner)

    def send_step(g):
        sender.start(step[g], step_p[g], pair_sem.at[g, 1], partner)

    def weight_grad(g):
        sender.wait(rows_p[g], pair_sem.at[g, 0])
        sender.wait(step_p[g], pair_sem.at[g, 1])
        tokens = rows_t[g].shape[-1]

        def body(i, col):
            left, left_p = rows_t[g][core].reshape(-1, tokens), rows_p[g][...].reshape(-1, tokens)
            right, right_p = step[g][:, col], step_p[g][:, col]
            if tokens % LANES == 0:
                total = dot(
                    jnp.concatenate([left, left_p], axis=1), jnp.concatenate([right, right_p], axis=0)
                )
            else:
                total = dot(left, right) + dot(left_p, right_p)
            mine[g][..., col] = total.reshape(mine[g].shape[:-1] + (TILE,)).astype(jnp.bfloat16)

        chunks(mine[g].shape[-1], body)

    from_x, from_y, line_x, line_y, line_u, line_d = (
        [None] + list(a) for a in (r.from_x, r.from_y, r.line_x, r.line_y, r.line_u, r.line_d)
    )
    lines = (line_u, line_d)
    half_sem, line_sem, chain_sem = r.half_sem, r.line_sem, r.chain_sem
    low, high = pl.ds(0, half), pl.ds(half, planes - half)

    def add(g, ys, xs, first, last, terms):
        depth = mine[g].shape[3]

        def body(i, carry):
            zs, at = first + i // depth, lax.rem(i, depth)
            total = mine[g][zs, ys, xs, at].astype(jnp.float32)
            for term, skip in terms:
                total = total + term[zs - skip, at].astype(jnp.float32)
            mine[g][zs, ys, xs, at] = total.astype(jnp.bfloat16)
            return carry

        lax.fori_loop(0, (last - first) * depth, body, 0)

    def scatter_stage(g, t):
        if t == 0:
            far = (1 - y, 1 - x)
            sender.start(mine[g].at[(low,) + far], from_x[g], half_sem.at[g, 0], across)
            sender.start(mine[g].at[(high,) + far], from_y[g], half_sem.at[g, 1], along)
            sender.start(mine[g].at[low, y, 1 - x], line_x[g].at[low], line_sem.at[g, 0], across)
            sender.start(mine[g].at[high, 1 - y, x], line_y[g].at[high], line_sem.at[g, 3], along)
        elif t == 1:
            sender.wait(from_y[g], half_sem.at[g, 1])
            add(g, y, 1 - x, half, planes, [(from_y[g], half)])
            sender.start(mine[g].at[high, y, 1 - x], line_x[g].at[high], line_sem.at[g, 1], across)
            sender.wait(from_x[g], half_sem.at[g, 0])
            add(g, 1 - y, x, 0, half, [(from_x[g], 0)])
            sender.start(mine[g].at[low, 1 - y, x], line_y[g].at[low], line_sem.at[g, 2], along)
        elif t == 2:
            sender.wait(line_x[g].at[low], line_sem.at[g, 0])
            sender.wait(line_x[g].at[high], line_sem.at[g, 1])
            sender.wait(line_y[g].at[low], line_sem.at[g, 2])
            sender.wait(line_y[g].at[high], line_sem.at[g, 3])
            add(g, y, x, 0, planes, [(line_x[g], 0), (line_y[g], 0)])
            chain(g, planes - 1)
        elif t == 3:
            for k in range(planes - 2, 1, -1):
                chain(g, k)
        elif t == 4:
            if planes > 2:
                chain(g, 1)
        else:
            land(g)

    def chain(g, k):
        for way, (at, inside, fed, target) in enumerate(
            ((z + k, z + k < planes, z > 0, up), (z - k, z - k >= 0, z < planes - 1, down))
        ):
            spot = jnp.clip(at, 0, planes - 1)

            @pl.when(both(inside, fed))
            def _(way=way, spot=spot):
                sender.wait(lines[way][g].at[spot], chain_sem.at[g, way, spot])

                def body(at, carry):
                    total = mine[g][spot, y, x, at].astype(jnp.float32)
                    total = total + lines[way][g][spot, at].astype(jnp.float32)
                    mine[g][spot, y, x, at] = total.astype(jnp.bfloat16)
                    return carry

                lax.fori_loop(0, mine[g].shape[3], body, 0)

            sender.start(
                mine[g].at[spot, y, x], lines[way][g].at[spot], chain_sem.at[g, way, spot], target, inside
            )

    def land(g):
        sender.wait(lines[0][g].at[z], chain_sem.at[g, 0, z], can_down)
        sender.wait(lines[1][g].at[z], chain_sem.at[g, 1, z], can_up)
        zero = jnp.zeros(mine[g].shape[4:], jnp.float32)

        def body(at, carry):
            total = mine[g][z, y, x, at].astype(jnp.float32)
            total = total + jnp.where(can_down, lines[0][g][z, at].astype(jnp.float32), zero)
            total = total + jnp.where(can_up, lines[1][g][z, at].astype(jnp.float32), zero)
            target, first = own[g]
            target[at, :, pl.ds(first, total.shape[1])] = total
            return carry

        lax.fori_loop(0, mine[g].shape[3], body, 0)

    held, got, small_sem = r.held, r.got, r.small_sem

    def small_pairs():
        for at, peer in enumerate((partner, across, along)):
            sender.start(held.at[at], got.at[at], small_sem.at[at], peer)
            sender.wait(got.at[at], small_sem.at[at])
            held[at + 1] = held[at] + got[at]
        for peer in others:
            sender.start(held.at[3], got.at[3 + z], small_sem.at[3 + z], peer)

    def small_land():
        for k in range(1, planes):
            at = lax.rem(z + k, planes)
            sender.wait(got.at[3 + at], small_sem.at[3 + at])
        got[3 + z] = held[3]
        total = got[3]
        for zs in range(1, planes):
            total = total + got[3 + zs]
        r.small_out[...] = total

    length_row, bucket_row, table = r.length, r.bucket, r.table
    rows_in, enc, cot = r.rows, r.enc, r.cot
    positions, width = rows_in.shape
    pairs = width // LANES
    hidden = r.hid.shape[1]
    gain = r.gain

    def onehot():
        ids = lax.broadcasted_iota(jnp.int32, (table.shape[0], positions), 0)
        return (ids == bucket_row[...]).astype(jnp.float32)

    def head_lanes(which):
        lane = lax.broadcasted_iota(jnp.int32, (1, LANES), 1) // HEAD
        return (lane == which).astype(jnp.bfloat16)

    def matmul(dst, source, g):
        def body(i, col):
            weight = whole[g][:, :, :, col].reshape(-1, TILE)
            dst[:, col] = dot(source[...], weight).astype(dst.dtype)

        chunks(whole[g].shape[-1], body)

    def matmul_back(source, g):
        acc = r.acc
        count = source.shape[0]
        acc[pl.ds(0, count), :] = jnp.zeros((count, width), jnp.float32)

        def body(i, col):
            weight = whole[g][:, :, :, col].reshape(-1, TILE)
            acc[pl.ds(0, count), :] += dot(source[:, col], weight, NT)

        chunks(whole[g].shape[-1], body)
        return acc[pl.ds(0, count), :]

    def norm_forward(value, which, dst, g):
        normed, unused = rms_parts(value)
        scaled = normed * gain[pl.ds(which, 1), :]
        dst[...] = scaled.astype(jnp.bfloat16)
        turn(g, scaled)
        send_rows(g)

    def norm_back(grad, value, which):
        normed, recip = rms_parts(value)
        scaled = grad * gain[pl.ds(which, 1), :]
        held[0, pl.ds(which, 1), :] = jnp.sum(grad * normed, axis=0, keepdims=True)
        return recip * (scaled - normed * jnp.mean(scaled * normed, axis=-1, keepdims=True))

    def per_pair(body):
        def run(j, carry):
            body(j, lambda base: pl.ds(pl.multiple_of(base + j * LANES, LANES), LANES))
            return carry

        lax.fori_loop(0, pairs, run, 0)

    def start_compute():
        gain[...] = jnp.sum(whole[GAIN][...].astype(jnp.float32), axis=(0, 1))
        spread = lax.dot_general(
            table[...], onehot(), TN, precision=lax.Precision.HIGHEST, preferred_element_type=jnp.float32
        )
        r.by_dist[pl.ds(0, spread.shape[0]), :] = spread
        norm_forward(rows_in[...].astype(jnp.float32), 0, r.h1, QKV)

    def early():
        turn(KVC, enc[...].astype(jnp.float32))
        send_rows(KVC)
        send_step(FFOUT)

    def self_attention():
        matmul(r.qkv, r.h1, QKV)
        row_ids = lax.broadcasted_iota(jnp.int32, (positions, positions), 0)
        col_ids = lax.broadcasted_iota(jnp.int32, (positions, positions), 1)
        qkv = r.qkv

        def body(j, at):
            live = (col_ids <= row_ids) & (col_ids < length_row[...])
            query, key, value = qkv[:, at(0)], qkv[:, at(width)], qkv[:, at(2 * width)]
            out = jnp.zeros((positions, LANES), jnp.float32)
            for e in range(2):
                lanes = head_lanes(e)
                head = 2 * j + e
                bias = jnp.broadcast_to(r.by_dist[pl.ds(head, 1), :], (positions, positions))
                bias = pltpu.roll(bias, 0, 1, stride=1, stride_axis=0)
                scores = jnp.where(live, dot(query * lanes, key, NT) + bias, -1e30)
                top = jnp.max(scores, axis=-1, keepdims=True)
                lse = top + jnp.log(jnp.sum(jnp.exp(scores - top), axis=-1, keepdims=True))
                prob = jnp.exp(scores - lse)
                r.prob[head] = prob
                out = out + dot(prob.astype(jnp.bfloat16), value * lanes)
            r.att[:, at(0)] = out.astype(jnp.bfloat16)

        per_pair(body)
        turn(OUT, r.att[...].astype(jnp.float32))
        send_rows(OUT)

    def after_self():
        def body(i, col):
            weight = whole[OUT][:, :, :, col].reshape(-1, TILE)
            r.x1[:, col] = rows_in[:, col].astype(jnp.float32) + dot(r.att[...], weight)

        chunks(width, body)
        norm_forward(r.x1[...], 1, r.h2, QC)

    def cross_attention():
        matmul(r.kvc, enc, KVC)
        kvc = r.kvc

        def body(j, at):
            query, key, value = r.qc[:, at(0)], kvc[:, at(0)], kvc[:, at(width)]
            out = jnp.zeros((positions, LANES), jnp.float32)
            for e in range(2):
                lanes = head_lanes(e)
                scores = dot(query * lanes, key, NT)
                lse = jnp.log(jnp.sum(jnp.exp(scores), axis=-1, keepdims=True))
                prob = jnp.exp(scores - lse)
                r.prob_c[2 * j + e] = prob
                out = out + dot(prob.astype(jnp.bfloat16), value * lanes)
            r.att_c[:, at(0)] = out.astype(jnp.bfloat16)

        per_pair(body)
        turn(OUTC, r.att_c[...].astype(jnp.float32))
        send_rows(OUTC)

    def after_cross():
        def body(i, col):
            weight = whole[OUTC][:, :, :, col].reshape(-1, TILE)
            r.x2[:, col] = r.x1[:, col] + dot(r.att_c[...], weight)

        chunks(width, body)
        norm_forward(r.x2[...], 2, r.h3, FFIN)

    def feed():
        gate_up = r.gate_up
        matmul(gate_up, r.h3, FFIN)
        turned = rows_t[FFOUT]
        tall = turned.shape[2] * turned.shape[3]
        chips = TILE // (2 * tall)

        def body(i, col):
            up_col = pl.ds(pl.multiple_of(hidden + i * TILE, TILE), TILE)
            value, unused = gelu_and_slope(gate_up[:, col])
            product = value * gate_up[:, up_col]
            r.hid[:, col] = product.astype(jnp.bfloat16)
            flipped = jnp.transpose(product, (1, 0)).reshape((chips, 2) + turned.shape[2:])
            flipped = flipped.astype(jnp.bfloat16)
            turned[0, pl.ds(i * chips, chips)] = flipped[:, 0]
            turned[1, pl.ds(i * chips, chips)] = flipped[:, 1]

        chunks(hidden, body)
        send_rows(FFOUT)

    def feed_back():
        gate_up, change = r.gate_up, step[FFIN]
        tall = whole[FFOUT].shape[1] * SUB
        devices = TILE // tall

        def body(i, col):
            up_col = pl.ds(pl.multiple_of(hidden + i * TILE, TILE), TILE)
            weight = whole[FFOUT][pl.ds(i * devices, devices)].reshape(TILE, width)
            d_hidden = dot(cot[...], weight, NT)
            value, slope = gelu_and_slope(gate_up[:, col])
            change[:, col] = (d_hidden * gate_up[:, up_col] * slope).astype(jnp.bfloat16)
            change[:, up_col] = (d_hidden * value).astype(jnp.bfloat16)

        chunks(hidden, body)
        send_step(FFIN)

    def finish_forward():
        def body(i, col):
            weight = whole[FFOUT][:, :, :, col].reshape(-1, TILE)
            r.result[:, col] = (r.x2[:, col] + dot(r.hid[...], weight)).astype(jnp.bfloat16)

        chunks(width, body)

    def before_cross():
        back = norm_back(matmul_back(step[FFIN], FFIN), r.x2[...], 2)
        r.dx[...] = cot[...].astype(jnp.float32) + back
        step[OUTC][...] = r.dx[...].astype(jnp.bfloat16)
        send_step(OUTC)

    def cross_attention_back():
        d_att = matmul_back_rows(step[OUTC], OUTC)
        kvc = r.kvc

        def body(j, at):
            query, key, value = r.qc[:, at(0)], kvc[:, at(0)], kvc[:, at(width)]
            grad, out = d_att[:, at(0)], r.att_c[:, at(0)].astype(jnp.float32)
            grads = attend_pair_back(j, query, key, value, grad, out, r.prob_c, None)
            step[QC][:, at(0)] = grads[0].astype(jnp.bfloat16)
            step[KVC][:, at(0)] = grads[1].astype(jnp.bfloat16)
            step[KVC][:, at(width)] = grads[2].astype(jnp.bfloat16)

        per_pair(body)
        send_step(KVC)
        send_step(QC)

    def matmul_back_rows(source, g):
        r.d_att[...] = matmul_back(source, g)
        return r.d_att

    def attend_pair_back(j, query, key, value, grad, out, probs, spread):
        grad_b = grad.astype(jnp.bfloat16)
        d_query, d_key, d_value = 0.0, 0.0, 0.0
        for e in range(2):
            lanes = head_lanes(e)
            prob = probs[2 * j + e]
            inside = lax.broadcasted_iota(jnp.int32, (positions, LANES), 1) // HEAD == e
            delta = jnp.sum(jnp.where(inside, grad * out, 0.0), axis=-1, keepdims=True)
            d_prob = dot(grad_b * lanes, value, NT)
            d_score = prob * (d_prob - delta)
            if spread is not None:
                spread(2 * j + e, d_score)
            d_score_b = d_score.astype(jnp.bfloat16)
            d_value = d_value + dot(prob.astype(jnp.bfloat16), grad_b * lanes, TN)
            d_query = d_query + dot(d_score_b, key * lanes)
            d_key = d_key + dot(d_score_b, query * lanes, TN)
        return d_query, d_key, d_value

    def between():
        r.enc_grad[...] = matmul_back(step[KVC], KVC).astype(jnp.bfloat16)
        back = norm_back(matmul_back(step[QC], QC), r.x1[...], 1)
        r.dx[...] += back
        step[OUT][...] = r.dx[...].astype(jnp.bfloat16)
        send_step(OUT)

    def self_attention_back():
        d_att = matmul_back_rows(step[OUT], OUT)
        qkv = r.qkv
        row = lax.broadcasted_iota(jnp.int32, (SUB, positions), 0)

        def spread(head, d_score):
            total, count = d_score, positions // 2
            while count >= SUB:
                total = total[:count] + pltpu.roll(total[count:], positions - count, 1)
                count //= 2
            for bit in (4, 2, 1):
                total = jnp.where(
                    lax.rem(row // bit, 2) == 1, pltpu.roll(total, positions - bit, 1), total
                )
            r.by_dist[pl.ds(head, 1), :] = jnp.sum(total, axis=0, keepdims=True)

        def body(j, at):
            query, key, value = qkv[:, at(0)], qkv[:, at(width)], qkv[:, at(2 * width)]
            grad, out = d_att[:, at(0)], r.att[:, at(0)].astype(jnp.float32)
            grads = attend_pair_back(j, query, key, value, grad, out, r.prob, spread)
            for part in range(3):
                step[QKV][:, at(part * width)] = grads[part].astype(jnp.bfloat16)

        per_pair(body)
        send_step(QKV)

    def last():
        back = norm_back(matmul_back(step[QKV], QKV), rows_in[...].astype(jnp.float32), 0)
        r.input_grad[...] = (r.dx[...] + back).astype(jnp.bfloat16)
        sums = lax.dot_general(
            r.by_dist[...], onehot(), NT, precision=lax.Precision.HIGHEST,
            preferred_element_type=jnp.float32,
        )
        held[0, pl.ds(SUB, sums.shape[0]), pl.ds(0, sums.shape[1])] = sums

    held[0] = jnp.zeros(held.shape[1:], jnp.float32)
    r.by_dist[...] = jnp.zeros(r.by_dist.shape, jnp.float32)
    gathers = {GAIN: 0, QKV: 0, OUT: 2, QC: 2, KVC: 3, OUTC: 4, FFIN: 5, FFOUT: 7}
    ready = {
        GAIN: start_compute,
        QKV: self_attention,
        OUT: after_self,
        QC: lambda: matmul(r.qc, r.h2, QC),
        KVC: cross_attention,
        OUTC: after_cross,
        FFIN: feed,
    }
    for now in range(max(gathers.values()) + planes + 2):
        for g, begin in gathers.items():
            if 0 <= now - begin < planes + 2:
                gather_stage(g, now - begin)
        if now == 0:
            early()
        for g, begin in gathers.items():
            if now - begin == planes + 1 and g != FFOUT:
                settle(g)
                ready[g]()
    weight_grad(FFOUT)
    settle(FFOUT)
    slots = [
        (feed_back, FFOUT),
        (before_cross, None),
        (lambda: weight_grad(FFIN), FFIN),
        (finish_forward, None),
        (cross_attention_back, None),
        (lambda: weight_grad(OUTC), OUTC),
        (between, None),
        (lambda: (weight_grad(KVC), weight_grad(QC)), (KVC, QC)),
        (self_attention_back, None),
        (lambda: weight_grad(OUT), OUT),
        (last, None),
        (lambda: weight_grad(QKV), QKV),
        (small_pairs, None),
    ]
    after = {
        1: [(FFOUT, 1)],
        3: [(FFOUT, 2)],
        5: [(FFOUT, 3)],
        6: [(FFIN, 1), (FFOUT, 4)],
        8: [(OUTC, 1), (FFOUT, 5)],
        10: [(FFIN, 2)],
        11: [(KVC, 1), (QC, 1)],
    }
    tail = [
        [(OUTC, 2), (FFIN, 3)],
        [(OUT, 1), (QKV, 1), (OUTC, 3), (FFIN, 4)],
        [(KVC, 2), (QC, 2), (OUTC, 4), (FFIN, 5)],
        [(OUT, 2), (KVC, 3), (QC, 3), (OUTC, 5)],
        [(QKV, 2), (OUT, 3), (KVC, 4), (QC, 4)],
        [(QKV, 3), (OUT, 4), (KVC, 5), (QC, 5)],
        [(QKV, 4), (OUT, 5)],
        [(QKV, 5)],
    ]
    def scatter_steps(batch):
        for g, t in batch:
            scatter_stage(g, t)

    scatter_stage(FFOUT, 0)
    for now, (work, groups) in enumerate(slots):
        work()
        if groups is not None and groups != FFOUT:
            for g in groups if isinstance(groups, tuple) else (groups,):
                scatter_stage(g, 0)
        scatter_steps(after.get(now, []))
    for batch in tail:
        scatter_steps(batch)
    small_land()
    sender.finish()


def per_device(
    inputs, encoded, lengths, bucket_ids, qkv_weights, out_weights, ff_in, ff_out, gains, bias_table, cotangent
):
    count = lax.axis_size("fsdp")
    me = lax.axis_index("fsdp")
    planes = count // 8
    half = planes // 2
    depth, width, hidden = qkv_weights.shape[0], qkv_weights.shape[-1], ff_in.shape[-1]
    positions, keys = inputs.shape[1], encoded.shape[1]
    heads, buckets = bias_table.shape[1], bias_table.shape[0]
    gain_row = lax.dynamic_update_slice(
        jnp.zeros((SUB, width), jnp.bfloat16), gains, (jnp.int32(0), me * gains.shape[1])
    )
    shards = [
        gain_row,
        qkv_weights.reshape(depth, 6 * width),
        out_weights.reshape(depth, 2 * width),
        ff_in.reshape(depth, 2 * hidden),
        ff_out,
    ]
    shards = [s.reshape(-1, SUB, s.shape[-1]) for s in shards]
    deep, tall = depth // SUB, ff_out.shape[0] // SUB
    widths = [width, 3 * width, width, width, 2 * width, width, 2 * hidden, width]
    deeps = [1] + [deep] * 6 + [tall]
    blocks = [(d, SUB, w) for d, w in zip(deeps, widths)]
    backward_ids = jnp.concatenate([bucket_ids[:1], bucket_ids[:0:-1]])[None]
    length_row = jnp.broadcast_to(lengths[:, None], (1, positions))
    bf, fl = jnp.bfloat16, jnp.float32
    any_spec, vmem = pl.BlockSpec(memory_space=pl.ANY), pl.BlockSpec(memory_space=pltpu.VMEM)
    ins = dict(
        shard=shards,
        rows=inputs[0],
        enc=encoded[0],
        cot=cotangent[0],
        length=length_row,
        bucket=backward_ids,
        table=bias_table,
    )
    in_specs = [any_spec if s.ndim == 3 else vmem for s in jax.tree.leaves(ins)]
    padded = 2 * SUB * -(-heads // (2 * SUB))
    small = (SUB + padded, width)
    square = (positions, width)
    kinds = range(1, 8)
    shape = jax.ShapeDtypeStruct
    outs = dict(
        result=shape(square, bf),
        input_grad=shape(square, bf),
        enc_grad=shape((keys, width), bf),
        small_out=shape(small, fl),
        own=[shape(s.shape, fl) for s in shards[1:]],
    )
    room, sems = pltpu.VMEM, pltpu.SemaphoreType.DMA
    tokens = [keys if g == KVC else positions for g in range(8)]
    chips = count // 2

    def rows_room(lead, g):
        return room(lead + (chips, blocks[g][0], SUB, tokens[g]), bf)

    def block_rooms(*lead):
        return [room(lead + blocks[g], bf) for g in kinds]

    rooms = dict(
        whole=[room((count,) + b, bf) for b in blocks],
        turned=[rows_room((2,), g) for g in kinds],
        turned_p=[rows_room((), g) for g in kinds],
        step=[room((tokens[g], blocks[g][2]), bf) for g in kinds if g != FFOUT],
        step_p=[room((tokens[g], blocks[g][2]), bf) for g in kinds],
        mine=block_rooms(planes, 2, 2),
        from_x=block_rooms(half),
        from_y=block_rooms(planes - half),
        line_x=block_rooms(planes),
        line_y=block_rooms(planes),
        line_u=block_rooms(planes),
        line_d=block_rooms(planes),
        gain=room((SUB, width), fl),
        by_dist=room((padded, positions), fl),
        h1=room(square, bf),
        h2=room(square, bf),
        h3=room(square, bf),
        qkv=room((positions, 3 * width), bf),
        qc=room(square, bf),
        kvc=room((keys, 2 * width), bf),
        att=room(square, bf),
        att_c=room(square, bf),
        prob=room((heads, positions, positions), fl),
        prob_c=room((heads, positions, keys), fl),
        x1=room(square, fl),
        x2=room(square, fl),
        dx=room(square, fl),
        acc=room(square, fl),
        d_att=room(square, fl),
        gate_up=room((positions, 2 * hidden), fl),
        hid=room((positions, hidden), bf),
        held=room((4,) + small, fl),
        got=room((3 + planes,) + small, fl),
        local_sem=sems((8,)),
        send_sem=sems((8 * (24 * planes) + 7 * (4 + 2 * planes) + 16 + planes,)),
        recv_sem=sems((8, count)),
        pair_sem=sems((8, 2)),
        share_sem=sems((8, 2, planes)),
        half_sem=sems((8, 2)),
        line_sem=sems((8, 4)),
        chain_sem=sems((8, 2, planes)),
        small_sem=sems((3 + planes,)),
    )

    in_leaves, out_leaves, room_leaves = jax.tree.leaves(ins), jax.tree.leaves(outs), jax.tree.leaves(rooms)
    sizes = [len(in_leaves), len(out_leaves), len(room_leaves)]
    at = iter(range(sum(sizes)))
    order = {}
    for part in (ins, outs, rooms):
        order.update(jax.tree.map(lambda unused: next(at), part))
    numbers, tree = jax.tree.flatten(order)
    done = pl.pallas_call(
        lambda *refs: layer_kernel(planes, tree, *[refs[i] for i in numbers]),
        out_shape=out_leaves,
        in_specs=in_specs,
        out_specs=[vmem] * len(out_leaves),
        scratch_shapes=room_leaves,
        compiler_params=pltpu.CompilerParams(
            collective_id=0, has_side_effects=True, vmem_limit_bytes=62 * 1024 * 1024
        ),
        name="layer",
    )(*in_leaves)
    done = types.SimpleNamespace(**jax.tree.unflatten(jax.tree.structure(outs), done))
    result, dx, enc_grad, total = done.result, done.input_grad, done.enc_grad, done.small_out
    done = done.own
    o_qkv, o_out, o_in, o_down = (o.reshape(-1, o.shape[-1]) for o in done)
    s_gain = lax.dynamic_slice(
        total[: gains.shape[0]], (jnp.int32(0), me * gains.shape[1]), gains.shape
    )
    s_table = jnp.transpose(total[SUB : SUB + heads, :buckets])
    return (
        result[None],
        dx[None],
        enc_grad[None],
        o_qkv.reshape(qkv_weights.shape),
        o_out.reshape(out_weights.shape),
        o_in.reshape(ff_in.shape),
        o_down,
        s_gain,
        s_table,
    )


def solution(mesh):
    count = mesh.shape["fsdp"]

    def layer(*args):
        depth, tall = args[4].shape[0], args[7].shape[0]
        tiled = depth % SUB == 0 and tall % SUB == 0 and count % 8 == 0 and count > 8
        tiled = tiled and TILE % (2 * tall) == 0 and args[0].shape[1] == LANES and LANES == 2 * HEAD
        return (per_device if tiled else plain_device)(*args)

    rows, split = P("fsdp", None, None), P("fsdp", None)
    return jax.shard_map(
        layer,
        mesh=mesh,
        in_specs=(rows, rows, P("fsdp"), P(), rows, rows, rows, split, P(None, "fsdp"), P(), rows),
        out_specs=(rows, rows, rows, rows, rows, rows, split, P(None, "fsdp"), P()),
        check_vma=False,
    )
```
